128 devices in a mesh: chan: 4 (over z), rows: 32 (over y, x, core).
Axes of the slice: x: 4, y: 4, z: 4, core: 2. Of those that a mesh axis runs over, the one named last changes fastest.
Arguments:
- estimate: float32 [4, 2048, 2048], P('chan', 'rows'), may hold values from -3 to 3
- dirty_image: float32 [4, 2048, 2048], P('chan', 'rows'), may hold values from -40 to 40
- psf_weights: float32 [4, 2048, 2048], P('chan', None, 'rows'), may hold values from 0.05 to 2
Outputs:
- new_estimate: float32 [4, 2048, 2048], P('chan', 'rows')
- residual: float32 [4, 2048, 2048], P('chan', 'rows')
The draws below stay inside these ranges and needn't reach their ends.
All inputs are finite; a program needn't handle non-finite values.
Results may differ from the reference program's by a relative error of at most 0.0001.
Values sent between devices are 32-bit elements; how exact they have to be, the bound alone decides.
A program may use at most 64 MiB of HBM per device.

```python
import jax
import jax.numpy as jnp
from jax import lax

N = 2048
CH = 4


def draw_dirty_image(key, part):
    key_list = jax.random.split(key, 3)
    noise_part = jax.random.normal(key_list[0], (CH, N, N), jnp.float32)
    row_log = jax.random.uniform(key_list[1], (N,), jnp.float32) - 0.5
    col_log = jax.random.uniform(key_list[2], (N,), jnp.float32) - 0.5
    position = jnp.arange(N, dtype=jnp.float32) / N - 0.5
    channel = jnp.arange(CH, dtype=jnp.float32) / (CH - 1) - 0.5
    rise_factor = 3.0
    scaling = (10.0 ** row_log)[:, None] * (10.0 ** col_log)[None, :] * (rise_factor ** position)[:, None]
    values = noise_part * scaling[None] * (3.0 ** channel)[:, None, None]
    return jnp.clip(values, -40.0, 40.0)


def shard_levels(own_key, dims, cuts, smallest, top_value):
    level, own = 1.0, jax.random.fold_in(own_key, 6)
    for dim, parts in cuts:
        steps = jnp.exp(jax.random.uniform(jax.random.fold_in(own, dim), (parts,), jnp.float32, smallest / len(cuts), top_value / len(cuts)))
        level = level * jnp.repeat(steps, dims[dim] // parts).reshape([-1 if axis == dim else 1 for axis in range(len(dims))])
    return level


def scatter_about(own_key, extent, deviation, bound, cuts=(), held_as=jnp.bfloat16):
    gain = shard_levels(own_key, extent, cuts, -0.22, 0.18) if cuts else 1.0
    drawn = jax.random.normal(own_key, extent, jnp.float32) * deviation * gain
    return jnp.minimum(jnp.maximum(drawn, -bound), bound).astype(held_as)


def setup_inputs(seed: int = 0) -> dict:
    arg_keys = jax.random.split(jax.random.key(seed), 4)
    estimate = scatter_about(arg_keys[0], (CH, N, N), 0.5, 3.0, ((0, 4), (1, 32)), jnp.float32)
    dirty_image = draw_dirty_image(jax.random.fold_in(arg_keys[3], 71), 0)
    psf_weights = jnp.clip(0.05 + 1.95 * jax.random.uniform(arg_keys[2], (CH, N, N), jnp.float32) ** shard_levels(arg_keys[2], (CH, N, N), ((0, 4), (2, 32)), -0.2, 0.2), 0.05, 2.0)
    return dict(estimate=estimate, dirty_image=dirty_image, psf_weights=psf_weights)


fractions = (0.03, 0.02, 0.015)
taps = (0.0625, 0.25, 0.375, 0.25, 0.0625)
step_size = 0.9

def psf_apply(values, weights):
    spectrum = jnp.fft.fft2(values)
    return jnp.real(jnp.fft.ifft2(spectrum * weights)).astype(values.dtype)

def smooth(values, spacing):
    count = values.shape[2]
    padded = jnp.pad(values, ((0, 0), (0, 0), (2 * spacing, 2 * spacing)))
    across = taps[0] * padded[:, :, 0:count]
    for tap_index in range(1, 5):
        across = across + taps[tap_index] * padded[:, :, tap_index * spacing:tap_index * spacing + count]
    height = values.shape[1]
    padded = jnp.pad(across, ((0, 0), (2 * spacing, 2 * spacing), (0, 0)))
    result = taps[0] * padded[:, 0:height]
    for tap_index in range(1, 5):
        result = result + taps[tap_index] * padded[:, tap_index * spacing:tap_index * spacing + height]
    return result

def reference(estimate, dirty_image, psf_weights):
    blurred = psf_apply(estimate, psf_weights)
    residual = dirty_image - blurred
    halfway = estimate + step_size * residual
    current = halfway
    details = []
    for scale_level in range(3):
        smoother = smooth(current, 1 << scale_level)
        details.append(current - smoother)
        current = smoother
    output = current
    for scale_level in range(3):
        detail = details[scale_level]
        energy = lax.optimization_barrier(jnp.sum(detail * detail, axis=0))
        peak = jnp.sqrt(jnp.max(energy))
        threshold = fractions[scale_level] * peak
        factor = 1.0 - threshold / jnp.maximum(jnp.sqrt(energy), threshold)
        output = output + factor[None] * detail
    return (output, residual)
```

```python
import functools
import math

import jax
import jax.numpy as jnp
import numpy as np
from jax import lax
from jax.experimental import pallas as pl
from jax.experimental.pallas import tpu as pltpu
from jax.sharding import PartitionSpec as P

fractions = (0.03, 0.02, 0.015)
step_size = 0.9
MESH = pl.DeviceIdType.MESH
F32 = jnp.float32
BF16 = jnp.bfloat16
R = 32
Z = 4
TILES = 5


def linear(pairs):
    total = None
    for coef, value in pairs:
        if abs(coef) < 1e-12:
            continue
        if abs(coef - 1.0) < 1e-12:
            total = value if total is None else total + value
        elif abs(coef + 1.0) < 1e-12:
            total = -value if total is None else total - value
        else:
            term = coef * value
            total = term if total is None else total + term
    return total


def cosine_16(first, middle, e):
    out = [None] * 9
    for k in range(5):
        even = linear(
            [(1.0, first), (1.0 if k % 2 == 0 else -1.0, middle)]
            + [(math.cos(2 * math.pi * k * a / 16), e[a]) for a in (2, 4, 6)]
        )
        odd = linear([(math.cos(2 * math.pi * k * a / 16), e[a]) for a in (1, 3, 5, 7)])
        if odd is None:
            out[k] = even
            out[8 - k] = even
        else:
            out[k] = even + odd
            out[8 - k] = even - odd
    return out


def sine_16(o):
    out = [None] * 8
    for k in range(1, 5):
        even = linear([(math.sin(2 * math.pi * k * a / 16), o[a]) for a in (2, 4, 6)])
        odd = linear([(math.sin(2 * math.pi * k * a / 16), o[a]) for a in (1, 3, 5, 7)])
        if even is None:
            out[k] = odd
        else:
            out[k] = odd + even
            out[8 - k] = odd - even
    return out


def fft(values, sign):
    count = len(values)
    if count == 1:
        return values
    if count == 2:
        (ar, ai), (br, bi) = values
        return [(ar + br, ai + bi), (ar - br, ai - bi)]
    if count == 4:
        (ar, ai), (br, bi), (cr, ci), (dr, di) = values
        sr, si, tr, ti = ar + cr, ai + ci, ar - cr, ai - ci
        ur, ui, vr, vi = br + dr, bi + di, br - dr, bi - di
        if sign > 0:
            return [(sr + ur, si + ui), (tr - vi, ti + vr), (sr - ur, si - ui), (tr + vi, ti - vr)]
        return [(sr + ur, si + ui), (tr + vi, ti - vr), (sr - ur, si - ui), (tr - vi, ti + vr)]
    quarter = count // 4
    parts = [fft(values[n::4], sign) for n in range(4)]
    out = [None] * count
    for k in range(quarter):
        four = []
        for n in range(4):
            re, im = parts[n][k]
            angle = sign * 2 * math.pi * n * k / count
            c, s = math.cos(angle), math.sin(angle)
            if n * k == 0:
                four.append((re, im))
            elif abs(abs(c) - abs(s)) < 1e-9:
                h = abs(c)
                cs, ss = math.copysign(1, c), math.copysign(1, s)
                r = (re if cs > 0 else -re) - (im if ss > 0 else -im)
                i = (im if cs > 0 else -im) + (re if ss > 0 else -re)
                four.append((h * r, h * i))
            else:
                four.append((re * c - im * s, re * s + im * c))
        for m, value in enumerate(fft(four, sign)):
            out[k + m * quarter] = value
    return out


def split(value):
    high = value.astype(BF16)
    return high, (value - high.astype(F32)).astype(BF16)


def dot3(a, b, dims):
    (ah, al), (bh, bl) = a, b
    dot = functools.partial(
        lax.dot_general, dimension_numbers=(dims, ((), ())), preferred_element_type=F32
    )
    return dot(ah, bh) + (dot(al, bh) + dot(ah, bl))


def tables():
    m = np.arange(128)
    rows = np.zeros((256, 256))
    for d in range(32):
        for jj in range(4):
            angle = 2 * np.pi * ((4 * d + jj) * m % 128) / 128
            rows[8 * d + jj] = np.concatenate([np.cos(angle), np.sin(angle)])
            rows[8 * d + 4 + jj] = np.concatenate([-np.sin(angle), np.cos(angle)])
    n = np.arange(64)
    angle = 2 * np.pi * (n[:, None] * n[None, :] % 64) / 64
    cols = np.zeros((2, 2, 64, 2, 2, 64))
    for kk in range(2):
        cols[0, kk, :, 0, kk] = np.cos(angle)
        cols[1, kk, :, 0, kk] = np.sin(angle)
        cols[0, kk, :, 1, kk] = -np.sin(angle)
        cols[1, kk, :, 1, kk] = np.cos(angle)
    cols = cols.reshape(256, 256)
    k = np.arange(1, 9)
    angle = -2 * np.pi * k[:, None] * m[None, :] / 2048
    row_twist = np.concatenate([np.cos(angle), np.sin(angle)])
    u1 = np.arange(32)
    angle = -2 * np.pi * u1[:, None] * n[None, :] / 2048
    angle = np.concatenate([angle, angle], axis=1)
    col_twist = np.stack([np.cos(angle), np.sin(angle)])

    def halves(table):
        high = table.astype(BF16)
        return np.stack([high, (table - high.astype(np.float64)).astype(BF16)])

    return (
        halves(rows),
        halves(cols),
        halves(cols.T),
        np.asarray(row_twist, np.float32),
        np.asarray(col_twist, np.float32),
    )


def roll(value, shift, axis):
    return pltpu.roll(value, shift % value.shape[axis], axis)


def smooth(value, spacing):
    for axis in (1, 0):
        value = value + roll(value, spacing, axis)
        value = value + roll(value, -spacing, axis)
        value = value + roll(value, spacing, axis)
        value = value + roll(value, -spacing, axis)
    return value * (1.0 / 256.0)


def kernel(
    est, dirty, weights, row_table, col_table, col_back, row_twist, col_twist,
    new_ref, res_ref,
    abuf, send, recv, spec, send2, recv2, hz, hr, det, energy, ob, mx_own, mx_z, mx_r,
    s_send, s_recv, s_send2, s_recv2, z_send, z_recv, h_send, h_recv, o_send, o_recv,
    mz_send, mz_recv, mr_send, mr_recv, own_sem,
):
    z = lax.axis_index("chan")
    p = lax.axis_index("rows")

    barrier = pltpu.get_barrier_semaphore()

    def greet_row(i, carry):
        pl.semaphore_signal(
            barrier, inc=1, device_id={"rows": lax.rem(p + i, R)}, device_id_type=MESH
        )
        return carry

    def greet_chan(i, carry):
        pl.semaphore_signal(
            barrier, inc=1, device_id={"chan": lax.rem(z + i, Z)}, device_id_type=MESH
        )
        return carry

    lax.fori_loop(1, R, greet_row, 0)
    lax.fori_loop(1, Z, greet_chan, 0)

    abuf[576:640, :] = jnp.zeros((64, 256), F32)

    def rows_forward(g, carry):
        at = pl.ds(pl.multiple_of(8 * g, 8), 8)
        x = [est[at, 128 * a : 128 * a + 128] for a in range(16)]
        e = [None] + [x[a] + x[16 - a] for a in range(1, 8)]
        o = [None] + [x[a] - x[16 - a] for a in range(1, 8)]
        re = cosine_16(x[0], x[8], e)
        im = sine_16(o)
        for k in range(1, 9):
            c = row_twist[k - 1 : k, :]
            s = row_twist[k + 7 : k + 8, :]
            to = pl.ds(pl.multiple_of(64 * (k - 1) + 8 * g, 8), 8)
            if k < 8:
                abuf[to, 0:128] = re[k] * c + im[k] * s
                abuf[to, 128:256] = re[k] * s - im[k] * c
            else:
                abuf[to, 0:128] = re[k] * c
                abuf[to, 128:256] = re[k] * s
        to = pl.ds(pl.multiple_of(512 + 8 * g, 8), 8)
        abuf[to, 0:128] = re[0]
        abuf[to, 128:256] = jnp.zeros((8, 128), F32)
        return carry

    lax.fori_loop(0, 8, rows_forward, 0)
    table = (row_table[0], row_table[1])
    for t in range(TILES):
        out = dot3(table, split(abuf[128 * t : 128 * t + 128, :]), ((1,), (1,)))
        send[:, t] = out.reshape(R, 8, 128)

    pl.semaphore_wait(barrier, R - 1 + Z - 1)

    def exchange(source, target, send_sem, recv_sem):
        def copy(to, slot, sem):
            return pltpu.make_async_remote_copy(
                src_ref=source.at[to],
                dst_ref=target.at[slot, 0:TILES],
                send_sem=send_sem.at[to],
                recv_sem=recv_sem.at[sem],
                device_id={"rows": to},
                device_id_type=MESH,
            )

        def begin(i, carry):
            copy(lax.rem(p + i, R), p, p).start()
            return carry

        lax.fori_loop(1, R, begin, 0)
        own = pltpu.make_async_copy(source.at[p], target.at[p, 0:TILES], own_sem)
        own.start()

        def end(i, carry):
            other = lax.rem(p + R - i, R)
            copy(other, other, other).wait_recv()
            return carry

        lax.fori_loop(1, R, end, 0)
        own.wait()

        def sent(i, carry):
            to = lax.rem(p + i, R)
            copy(to, p, p).wait_send()
            return carry

        lax.fori_loop(1, R, sent, 0)

    exchange(send, recv, s_send, s_recv)

    recv[:, TILES] = jnp.zeros((R, 8, 128), F32)
    upper = lax.broadcasted_iota(jnp.int32, (8, 128), 0) < 4

    def columns(q, carry):
        values = []
        for i in range(R):
            a = recv[i, 2 * q]
            b = recv[i, 2 * q + 1]
            values.append(
                (jnp.where(upper, a, roll(b, 4, 0)), jnp.where(upper, roll(a, 4, 0), b))
            )
        for u, (re, im) in enumerate(fft(values, -1)):
            c = col_twist[0, u : u + 1, :]
            s = col_twist[1, u : u + 1, :]
            spec[8 * u : 8 * u + 8, 0:128] = re * c - im * s
            spec[8 * u : 8 * u + 8, 128:256] = re * s + im * c
        out = dot3(split(spec[...]), (col_table[0], col_table[1]), ((1,), (0,)))
        w = weights[q].reshape(256, 128)
        out = jnp.concatenate([out[:, 0:128] * w, out[:, 128:256] * w], axis=1)
        spec[...] = dot3(split(out), (col_back[0], col_back[1]), ((1,), (0,)))
        values = []
        for u in range(R):
            c = col_twist[0, u : u + 1, :]
            s = col_twist[1, u : u + 1, :]
            re = spec[8 * u : 8 * u + 8, 0:128]
            im = spec[8 * u : 8 * u + 8, 128:256]
            values.append((re * c + im * s, im * c - re * s))
        for i, (re, im) in enumerate(fft(values, 1)):
            send2[i, 2 * q] = jnp.where(upper, re, roll(im, 4, 0))
            send2[i, 2 * q + 1] = jnp.where(upper, roll(re, 4, 0), im)
        return carry

    lax.fori_loop(0, 3, columns, 0)

    def copy2(to, slot, sem):
        return pltpu.make_async_remote_copy(
            src_ref=send2.at[to, 0:TILES],
            dst_ref=recv2.at[slot],
            send_sem=s_send2.at[to],
            recv_sem=s_recv2.at[sem],
            device_id={"rows": to},
            device_id_type=MESH,
        )

    def begin2(i, carry):
        copy2(lax.rem(p + i, R), p, p).start()
        return carry

    lax.fori_loop(1, R, begin2, 0)
    own2 = pltpu.make_async_copy(send2.at[p, 0:TILES], recv2.at[p], own_sem)
    own2.start()

    def end2(i, carry):
        other = lax.rem(p + R - i, R)
        copy2(other, other, other).wait_recv()
        return carry

    lax.fori_loop(1, R, end2, 0)
    own2.wait()

    for t in range(TILES):
        block = recv2[:, t].reshape(256, 128)
        abuf[128 * t : 128 * t + 128, :] = dot3(split(block), table, ((0,), (0,)))

    for c in range(Z):
        if c == 0:
            hz[c, :, 0:128] = jnp.zeros((64, 128), F32)
        if c == Z - 1:
            hz[c, :, 640:768] = jnp.zeros((64, 128), F32)

    def rows_inverse(g, carry):
        re, im = [None] * 9, [None] * 8
        for k in range(1, 9):
            c = row_twist[k - 1 : k, :]
            s = row_twist[k + 7 : k + 8, :]
            to = pl.ds(pl.multiple_of(64 * (k - 1) + 8 * g, 8), 8)
            gr, gi = abuf[to, 0:128], abuf[to, 128:256]
            re[k] = gr * c + gi * s
            if k < 8:
                im[k] = gi * c - gr * s
        re[0] = abuf[pl.ds(pl.multiple_of(512 + 8 * g, 8), 8), 0:128]
        cosine = cosine_16(re[0], re[8], re)
        sine = sine_16(im)
        at = pl.ds(pl.multiple_of(8 * g, 8), 8)
        for a in range(16):
            if a == 0 or a == 8:
                blurred = cosine[a]
            elif a < 8:
                blurred = cosine[a] - sine[a]
            else:
                blurred = cosine[16 - a] + sine[16 - a]
            lanes = slice(128 * a, 128 * a + 128)
            residual = dirty[at, lanes] - blurred
            res_ref[at, lanes] = residual
            halfway = est[at, lanes] + step_size * residual
            own = a // 4
            hz[own, at, 128 * (a % 4) + 128 : 128 * (a % 4) + 256] = halfway
            if a % 4 == 0 and own > 0:
                hz[own - 1, at, 640:768] = halfway
            if a % 4 == 3 and own < Z - 1:
                hz[own + 1, at, 0:128] = halfway
        return carry

    lax.fori_loop(0, 8, rows_inverse, 0)

    def copy_z(to, slot, sem):
        return pltpu.make_async_remote_copy(
            src_ref=hz.at[to],
            dst_ref=hr.at[slot, 16:80, :],
            send_sem=z_send.at[to],
            recv_sem=z_recv.at[sem],
            device_id={"chan": to},
            device_id_type=MESH,
        )

    for i in range(1, Z):
        copy_z(lax.rem(z + i, Z), z, z).start()
    own3 = pltpu.make_async_copy(hz.at[z], hr.at[z, 16:80, :], own_sem)
    own3.start()

    @pl.when(p == 0)
    def _():
        hr[:, 0:16, :] = jnp.zeros((Z, 16, 768), F32)

    @pl.when(p == R - 1)
    def _():
        hr[:, 80:96, :] = jnp.zeros((Z, 16, 768), F32)

    for i in range(1, Z):
        other = lax.rem(z + Z - i, Z)
        copy_z(other, other, other).wait_recv()
    own3.wait()

    above = pltpu.make_async_remote_copy(
        src_ref=hr.at[:, 16:32, :],
        dst_ref=hr.at[:, 80:96, :],
        send_sem=h_send.at[0],
        recv_sem=h_recv.at[0],
        device_id={"rows": lax.rem(p + R - 1, R)},
        device_id_type=MESH,
    )
    below = pltpu.make_async_remote_copy(
        src_ref=hr.at[:, 64:80, :],
        dst_ref=hr.at[:, 0:16, :],
        send_sem=h_send.at[1],
        recv_sem=h_recv.at[1],
        device_id={"rows": lax.rem(p + 1, R)},
        device_id_type=MESH,
    )

    @pl.when(p > 0)
    def _():
        above.start()

    @pl.when(p < R - 1)
    def _():
        below.start()

    @pl.when(p < R - 1)
    def _():
        above.wait_recv()

    @pl.when(p > 0)
    def _():
        below.wait_recv()

    row_ids = lax.broadcasted_iota(jnp.int32, (96, 1), 0) + 64 * p - 16
    col_ids = lax.broadcasted_iota(jnp.int32, (1, 768), 1) + 512 * z - 128
    row_mask = jnp.logical_and(row_ids >= 0, row_ids < 64 * R).astype(F32)
    col_mask = jnp.logical_and(col_ids >= 0, col_ids < 512 * Z).astype(F32)

    def starlet(ch, carry):
        current = hr[ch]
        for level in range(3):
            later = smooth(current, 1 << level)
            if level < 2:
                later = later * row_mask * col_mask
            detail = (current - later)[16:80, 128:640]
            det[level, ch] = detail
            squared = detail * detail
            energy[level] = jnp.where(ch == 0, squared, energy[level] + squared)
            current = later
        return carry

    energy[...] = jnp.zeros((3, 64, 512), F32)
    lax.fori_loop(0, Z, starlet, 0)

    lane = lax.broadcasted_iota(jnp.int32, (1, 128), 1)
    peaks = jnp.zeros((1, 128), F32)
    for level in range(3):
        peaks = jnp.where(lane == level, jnp.max(energy[level]), peaks)
    mx_own[0] = peaks

    def copy_mz(to, slot):
        return pltpu.make_async_remote_copy(
            src_ref=mx_own.at[0],
            dst_ref=mx_z.at[slot],
            send_sem=mz_send.at[to],
            recv_sem=mz_recv.at[slot],
            device_id={"chan": to},
            device_id_type=MESH,
        )

    for i in range(1, Z):
        copy_mz(lax.rem(z + i, Z), z).start()
    mx_z[z] = peaks
    for i in range(1, Z):
        other = lax.rem(z + Z - i, Z)
        copy_mz(other, other).wait_recv()
    peaks = jnp.max(mx_z[...], axis=0)
    mx_own[1] = peaks

    def copy_mr(to, slot):
        return pltpu.make_async_remote_copy(
            src_ref=mx_own.at[1],
            dst_ref=mx_r.at[slot],
            send_sem=mr_send.at[to],
            recv_sem=mr_recv.at[slot],
            device_id={"rows": to},
            device_id_type=MESH,
        )

    def begin_mr(i, carry):
        copy_mr(lax.rem(p + i, R), p).start()
        return carry

    lax.fori_loop(1, R, begin_mr, 0)
    mx_r[p] = peaks
    energy[...] = lax.rsqrt(energy[...])

    def end_mr(i, carry):
        other = lax.rem(p + R - i, R)
        copy_mr(other, other).wait_recv()
        return carry

    lax.fori_loop(1, R, end_mr, 0)
    peaks = jnp.sqrt(jnp.max(mx_r[...], axis=0))
    thresholds = [
        fractions[level] * jnp.max(jnp.where(lane == level, peaks, 0.0)) for level in range(3)
    ]
    for level in range(3):
        energy[level] = jnp.minimum(energy[level] * thresholds[level], 1.0)

    def copy_o(to, slot, sem):
        return pltpu.make_async_remote_copy(
            src_ref=ob.at[to],
            dst_ref=new_ref.at[:, pl.ds(pl.multiple_of(512 * slot, 512), 512)],
            send_sem=o_send.at[to],
            recv_sem=o_recv.at[sem],
            device_id={"chan": to},
            device_id_type=MESH,
        )

    def final(i, carry):
        ch = lax.rem(z + i, Z)
        out = hr[ch, 16:80, 128:640]
        for level in range(3):
            out = out - energy[level] * det[level, ch]
        ob[ch] = out
        copy_o(ch, z, z).start()
        return carry

    lax.fori_loop(1, Z, final, 0)
    out = hr[z, 16:80, 128:640]
    for level in range(3):
        out = out - energy[level] * det[level, z]
    new_ref[:, pl.ds(pl.multiple_of(512 * z, 512), 512)] = out

    def sent2(i, carry):
        to = lax.rem(p + i, R)
        copy2(to, p, p).wait_send()
        copy_mr(to, p).wait_send()
        return carry

    lax.fori_loop(1, R, sent2, 0)

    @pl.when(p > 0)
    def _():
        above.wait_send()

    @pl.when(p < R - 1)
    def _():
        below.wait_send()

    for i in range(1, Z):
        other = lax.rem(z + Z - i, Z)
        copy_o(other, other, other).wait_recv()
    for i in range(1, Z):
        to = lax.rem(z + i, Z)
        copy_z(to, z, z).wait_send()
        copy_mz(to, z).wait_send()
        copy_o(to, z, z).wait_send()


def arrange_weights(w):
    other = lax.ppermute(w, "rows", [(i, R - 1 - i) for i in range(R)])
    mirror = jnp.roll(jnp.flip(other, axis=0), 1, axis=0)
    mirror = jnp.roll(jnp.flip(mirror, axis=1), 1, axis=1)
    w4 = w.reshape(64, 32, 4, 16)
    m4 = mirror.reshape(64, 32, 4, 16)
    both = jnp.concatenate(
        [
            w4[..., 1:8] + m4[..., 1:8],
            w4[..., 8:9],
            w4[..., 0:1],
            jnp.zeros((64, 32, 4, 3), F32),
        ],
        axis=3,
    ) * (1.0 / (2048.0 * 2048.0))
    both = both.reshape(64, 32, 4, 3, 2, 2)
    return both.transpose(3, 1, 4, 2, 5, 0).reshape(3, 32, 8, 128)


def shards(estimate, dirty_image, psf_weights):
    weights = arrange_weights(psf_weights[0])
    constants = tables()
    vmem = pl.BlockSpec(memory_space=pltpu.VMEM)
    block = jax.ShapeDtypeStruct((64, 2048), F32)
    dma = pltpu.SemaphoreType.DMA
    new, res = pl.pallas_call(
        kernel,
        out_shape=(block, block),
        in_specs=[vmem] * 8,
        out_specs=(vmem, vmem),
        scratch_shapes=[
            pltpu.VMEM((640, 256), F32),
            pltpu.VMEM((R, TILES, 8, 128), F32),
            pltpu.VMEM((R, TILES + 1, 8, 128), F32),
            pltpu.VMEM((256, 256), F32),
            pltpu.VMEM((R, TILES + 1, 8, 128), F32),
            pltpu.VMEM((R, TILES, 8, 128), F32),
            pltpu.VMEM((Z, 64, 768), F32),
            pltpu.VMEM((Z, 96, 768), F32),
            pltpu.VMEM((3, Z, 64, 512), F32),
            pltpu.VMEM((3, 64, 512), F32),
            pltpu.VMEM((Z, 64, 512), F32),
            pltpu.VMEM((2, 1, 128), F32),
            pltpu.VMEM((Z, 1, 128), F32),
            pltpu.VMEM((R, 1, 128), F32),
            dma((R,)), dma((R,)), dma((R,)), dma((R,)),
            dma((Z,)), dma((Z,)), dma((2,)), dma((2,)), dma((Z,)), dma((Z,)),
            dma((Z,)), dma((Z,)), dma((R,)), dma((R,)), dma,
        ],
        compiler_params=pltpu.CompilerParams(collective_id=0, has_side_effects=True),
    )(estimate[0], dirty_image[0], weights, *constants)
    return (new[None], res[None])


def solution(mesh):
    return jax.shard_map(
        shards,
        mesh=mesh,
        in_specs=(P("chan", "rows", None), P("chan", "rows", None), P("chan", None, "rows")),
        out_specs=(P("chan", "rows", None), P("chan", "rows", None)),
        check_vma=False,
    )
```

```python
import functools
import math

import jax
import jax.numpy as jnp
import numpy as np
from jax import lax
from jax.experimental import pallas as pl
from jax.experimental.pallas import tpu as pltpu
from jax.sharding import PartitionSpec as P

fractions = (0.03, 0.02, 0.015)
step_size = 0.9
MESH = pl.DeviceIdType.MESH
F32 = jnp.float32
BF16 = jnp.bfloat16
R = 32
Z = 4
TILES = 5


def linear(pairs):
    total = None
    for coef, value in pairs:
        if abs(coef) < 1e-12:
            continue
        if abs(coef - 1.0) < 1e-12:
            total = value if total is None else total + value
        elif abs(coef + 1.0) < 1e-12:
            total = -value if total is None else total - value
        else:
            term = coef * value
            total = term if total is None else total + term
    return total


def cosine_16(first, middle, e):
    out = [None] * 9
    for k in range(5):
        even = linear(
            [(1.0, first), (1.0 if k % 2 == 0 else -1.0, middle)]
            + [(math.cos(2 * math.pi * k * a / 16), e[a]) for a in (2, 4, 6)]
        )
        odd = linear([(math.cos(2 * math.pi * k * a / 16), e[a]) for a in (1, 3, 5, 7)])
        if odd is None:
            out[k] = even
            out[8 - k] = even
        else:
            out[k] = even + odd
            out[8 - k] = even - odd
    return out


def sine_16(o):
    out = [None] * 8
    for k in range(1, 5):
        even = linear([(math.sin(2 * math.pi * k * a / 16), o[a]) for a in (2, 4, 6)])
        odd = linear([(math.sin(2 * math.pi * k * a / 16), o[a]) for a in (1, 3, 5, 7)])
        if even is None:
            out[k] = odd
        else:
            out[k] = odd + even
            out[8 - k] = odd - even
    return out


def fft(values, sign):
    count = len(values)
    if count == 1:
        return values
    if count == 2:
        (ar, ai), (br, bi) = values
        return [(ar + br, ai + bi), (ar - br, ai - bi)]
    if count == 4:
        (ar, ai), (br, bi), (cr, ci), (dr, di) = values
        sr, si, tr, ti = ar + cr, ai + ci, ar - cr, ai - ci
        ur, ui, vr, vi = br + dr, bi + di, br - dr, bi - di
        if sign > 0:
            return [(sr + ur, si + ui), (tr - vi, ti + vr), (sr - ur, si - ui), (tr + vi, ti - vr)]
        return [(sr + ur, si + ui), (tr + vi, ti - vr), (sr - ur, si - ui), (tr - vi, ti + vr)]
    quarter = count // 4
    parts = [fft(values[n::4], sign) for n in range(4)]
    out = [None] * count
    for k in range(quarter):
        four = []
        for n in range(4):
            re, im = parts[n][k]
            angle = sign * 2 * math.pi * n * k / count
            c, s = math.cos(angle), math.sin(angle)
            if n * k == 0:
                four.append((re, im))
            elif abs(abs(c) - abs(s)) < 1e-9:
                h = abs(c)
                cs, ss = math.copysign(1, c), math.copysign(1, s)
                r = (re if cs > 0 else -re) - (im if ss > 0 else -im)
                i = (im if cs > 0 else -im) + (re if ss > 0 else -re)
                four.append((h * r, h * i))
            else:
                four.append((re * c - im * s, re * s + im * c))
        for m, value in enumerate(fft(four, sign)):
            out[k + m * quarter] = value
    return out


def split(value):
    high = value.astype(BF16)
    return high, (value - high.astype(F32)).astype(BF16)


def dot3(a, b, dims):
    (ah, al), (bh, bl) = a, b
    dot = functools.partial(
        lax.dot_general, dimension_numbers=(dims, ((), ())), preferred_element_type=F32
    )
    return dot(ah, bh) + (dot(al, bh) + dot(ah, bl))


def tables():
    m = np.arange(128)
    rows = np.zeros((256, 256))
    for d in range(32):
        for jj in range(4):
            angle = 2 * np.pi * ((4 * d + jj) * m % 128) / 128
            rows[8 * d + jj] = np.concatenate([np.cos(angle), np.sin(angle)])
            rows[8 * d + 4 + jj] = np.concatenate([-np.sin(angle), np.cos(angle)])
    n = np.arange(64)
    angle = 2 * np.pi * (n[:, None] * n[None, :] % 64) / 64
    cols = np.zeros((2, 2, 64, 2, 2, 64))
    for kk in range(2):
        cols[0, kk, :, 0, kk] = np.cos(angle)
        cols[1, kk, :, 0, kk] = np.sin(angle)
        cols[0, kk, :, 1, kk] = -np.sin(angle)
        cols[1, kk, :, 1, kk] = np.cos(angle)
    cols = cols.reshape(256, 256)
    k = np.arange(1, 9)
    angle = -2 * np.pi * k[:, None] * m[None, :] / 2048
    row_twist = np.concatenate([np.cos(angle), np.sin(angle)])
    u1 = np.arange(32)
    angle = -2 * np.pi * u1[:, None] * n[None, :] / 2048
    angle = np.concatenate([angle, angle], axis=1)
    col_twist = np.stack([np.cos(angle), np.sin(angle)])

    flip = np.zeros((2, 2, 128, 128))
    for kk in range(2):
        for u in range(64):
            flip[0, :, 64 * kk + 63 - u, 64 * kk + u] = 1.0
            flip[1, :, 64 * kk + (64 - u) % 64, 64 * kk + u] = 1.0
    pick = np.zeros((2, 40, 2, 64))
    for kk in range(2):
        for q in range(3):
            for half in range(2):
                s = 4 * q + 2 * half + kk
                k = s + 1 if s < 8 else 0
                for jj in range(4):
                    if s < 9:
                        pick[kk, 8 * q + 4 * half + jj, :, 16 * jj + k] = 2.0**-22
                    if s < 7:
                        pick[kk, 24 + 8 * q + 4 * half + jj, :, 16 * (3 - jj) + 16 - k] = 2.0**-22
    perm = np.concatenate([flip.reshape(512, 128), pick.reshape(80, 128)]).astype(BF16)

    def halves(table):
        high = table.astype(BF16)
        return np.stack([high, (table - high.astype(np.float64)).astype(BF16)])

    return (
        halves(rows),
        halves(cols),
        halves(cols.T),
        np.asarray(row_twist, np.float32),
        np.asarray(col_twist, np.float32),
        perm,
    )


def roll(value, shift, axis):
    return pltpu.roll(value, shift % value.shape[axis], axis)


def smooth(value, spacing):
    for axis in (1, 0):
        value = value + roll(value, spacing, axis)
        value = value + roll(value, -spacing, axis)
        value = value + roll(value, spacing, axis)
        value = value + roll(value, -spacing, axis)
    return value * (1.0 / 256.0)


def kernel(
    est, dirty, psf, row_table, col_table, col_back, row_twist, col_twist, perm,
    shrink_ref, blur_ref,
    abuf, send, recv, spec, send2, recv2, hz, hh, hp, hpr, hr, det, energy, ob, mx_own, mx_z, mx_r,
    weights, mirror, flipped, mirror_in, w_send, w_recv, p_send, p_recv,
    s_send, s_recv, s_send2, s_recv2, z_send, z_recv, h_send, h_recv, o_send, o_recv,
    mz_send, mz_recv, mr_send, mr_recv, own_sem,
):
    z = lax.axis_index("chan")
    p = lax.axis_index("rows")

    barrier = pltpu.get_barrier_semaphore()

    def greet_row(i, carry):
        pl.semaphore_signal(
            barrier, inc=1, device_id={"rows": lax.rem(p + i, R)}, device_id_type=MESH
        )
        return carry

    def greet_chan(i, carry):
        pl.semaphore_signal(
            barrier, inc=1, device_id={"chan": lax.rem(z + i, Z)}, device_id_type=MESH
        )
        return carry

    lax.fori_loop(1, R, greet_row, 0)
    lax.fori_loop(1, Z, greet_chan, 0)

    abuf[576:640, :] = jnp.zeros((64, 256), F32)

    def rows_forward(g, carry):
        at = pl.ds(pl.multiple_of(8 * g, 8), 8)
        x = [est[at, 128 * a : 128 * a + 128] for a in range(16)]
        e = [None] + [x[a] + x[16 - a] for a in range(1, 8)]
        o = [None] + [x[a] - x[16 - a] for a in range(1, 8)]
        re = cosine_16(x[0], x[8], e)
        im = sine_16(o)
        for k in range(1, 9):
            c = row_twist[k - 1 : k, :]
            s = row_twist[k + 7 : k + 8, :]
            to = pl.ds(pl.multiple_of(64 * (k - 1) + 8 * g, 8), 8)
            if k < 8:
                abuf[to, 0:128] = re[k] * c + im[k] * s
                abuf[to, 128:256] = re[k] * s - im[k] * c
            else:
                abuf[to, 0:128] = re[k] * c
                abuf[to, 128:256] = re[k] * s
        to = pl.ds(pl.multiple_of(512 + 8 * g, 8), 8)
        abuf[to, 0:128] = re[0]
        abuf[to, 128:256] = jnp.zeros((8, 128), F32)
        return carry

    lax.fori_loop(0, 8, rows_forward, 0)
    table = (row_table[0], row_table[1])
    for t in range(TILES):
        out = dot3(table, split(abuf[128 * t : 128 * t + 128, :]), ((1,), (1,)))
        send[:, t] = out.reshape(R, 8, 128)

    pl.semaphore_wait(barrier, R - 1 + Z - 1)

    partner = pltpu.make_async_remote_copy(
        src_ref=flipped,
        dst_ref=mirror_in,
        send_sem=w_send,
        recv_sem=w_recv,
        device_id={"rows": R - 1 - p},
        device_id_type=MESH,
    )
    left_half = lax.broadcasted_iota(jnp.int32, (40, 128), 1) < 64

    def arrange_weights():
        for i in range(8):
            rows = [psf[pl.ds(4 * i + n, 64, stride=32), :] for n in range(4)]
            high, low = split(jnp.concatenate(rows, axis=0))
            both = jnp.concatenate([high, low], axis=1)
            out = lax.dot_general(
                perm[512:592], both, (((1,), (1,)), ((), ())), preferred_element_type=F32
            )
            for n in range(2):
                a = out[0:40, 128 * n : 128 * n + 128]
                b = out[40:80, 128 * n : 128 * n + 128]
                first = jnp.where(left_half, a, roll(b, 64, 1))
                second = jnp.where(left_half, roll(a, 64, 1), b)
                for u1, value in ((4 * i + 2 * n, first), (4 * i + 2 * n + 1, second)):
                    for q in range(3):
                        weights[q, u1] = value[8 * q : 8 * q + 8]
                    for q in range(2):
                        mirror[q, u1] = value[24 + 8 * q : 32 + 8 * q]
        for q in range(2):
            high, low = split(mirror[q].reshape(256, 128))
            both = jnp.concatenate([high, low], axis=1)
            out = jnp.dot(both, perm[0:256], preferred_element_type=F32)
            zero = jnp.dot(both[0:16], perm[256:512], preferred_element_type=F32)
            flipped[q, 0] = zero[0:8]
            for u1 in range(1, 32):
                flipped[q, 32 - u1] = out[8 * u1 : 8 * u1 + 8]
        partner.start()

    def exchange(source, target, send_sem, recv_sem, between):
        def copy(to, slot, sem):
            return pltpu.make_async_remote_copy(
                src_ref=source.at[to],
                dst_ref=target.at[slot, 0:TILES],
                send_sem=send_sem.at[to],
                recv_sem=recv_sem.at[sem],
                device_id={"rows": to},
                device_id_type=MESH,
            )

        def begin(i, carry):
            copy(lax.rem(p + i, R), p, p).start()
            return carry

        lax.fori_loop(1, R, begin, 0)
        own = pltpu.make_async_copy(source.at[p], target.at[p, 0:TILES], own_sem)
        own.start()
        between()

        def end(i, carry):
            other = lax.rem(p + R - i, R)
            copy(other, other, other).wait_recv()
            return carry

        lax.fori_loop(1, R, end, 0)
        own.wait()

        def sent(i, carry):
            to = lax.rem(p + i, R)
            copy(to, p, p).wait_send()
            return carry

        lax.fori_loop(1, R, sent, 0)

    exchange(send, recv, s_send, s_recv, arrange_weights)
    partner.wait_recv()
    partner.wait_send()
    for q in range(2):
        weights[q] = weights[q] + mirror_in[q]

    recv[:, TILES] = jnp.zeros((R, 8, 128), F32)
    upper = lax.broadcasted_iota(jnp.int32, (8, 128), 0) < 4

    def columns(q, carry):
        values = []
        for i in range(R):
            a = recv[i, 2 * q]
            b = recv[i, 2 * q + 1]
            values.append(
                (jnp.where(upper, a, roll(b, 4, 0)), jnp.where(upper, roll(a, 4, 0), b))
            )
        for u, (re, im) in enumerate(fft(values, -1)):
            c = col_twist[0, u : u + 1, :]
            s = col_twist[1, u : u + 1, :]
            spec[8 * u : 8 * u + 8, 0:128] = re * c - im * s
            spec[8 * u : 8 * u + 8, 128:256] = re * s + im * c
        out = dot3(split(spec[...]), (col_table[0], col_table[1]), ((1,), (0,)))
        w = weights[q].reshape(256, 128)
        out = jnp.concatenate([out[:, 0:128] * w, out[:, 128:256] * w], axis=1)
        spec[...] = dot3(split(out), (col_back[0], col_back[1]), ((1,), (0,)))
        values = []
        for u in range(R):
            c = col_twist[0, u : u + 1, :]
            s = col_twist[1, u : u + 1, :]
            re = spec[8 * u : 8 * u + 8, 0:128]
            im = spec[8 * u : 8 * u + 8, 128:256]
            values.append((re * c + im * s, im * c - re * s))
        for i, (re, im) in enumerate(fft(values, 1)):
            send2[i, 2 * q] = jnp.where(upper, re, roll(im, 4, 0))
            send2[i, 2 * q + 1] = jnp.where(upper, roll(re, 4, 0), im)
        return carry

    lax.fori_loop(0, 3, columns, 0)

    def copy2(to, slot, sem):
        return pltpu.make_async_remote_copy(
            src_ref=send2.at[to, 0:TILES],
            dst_ref=recv2.at[slot],
            send_sem=s_send2.at[to],
            recv_sem=s_recv2.at[sem],
            device_id={"rows": to},
            device_id_type=MESH,
        )

    def begin2(i, carry):
        copy2(lax.rem(p + i, R), p, p).start()
        return carry

    lax.fori_loop(1, R, begin2, 0)
    own2 = pltpu.make_async_copy(send2.at[p, 0:TILES], recv2.at[p], own_sem)
    own2.start()

    def end2(i, carry):
        other = lax.rem(p + R - i, R)
        copy2(other, other, other).wait_recv()
        return carry

    lax.fori_loop(1, R, end2, 0)
    own2.wait()

    def sent2(i, carry):
        copy2(lax.rem(p + i, R), p, p).wait_send()
        return carry

    lax.fori_loop(1, R, sent2, 0)

    for t in range(TILES):
        block = recv2[:, t].reshape(256, 128)
        abuf[128 * t : 128 * t + 128, :] = dot3(split(block), table, ((0,), (0,)))

    left_lanes = lax.broadcasted_iota(jnp.int32, (8, 128), 1) < 64
    def rows_inverse(g, carry):
        re, im = [None] * 9, [None] * 8
        for k in range(1, 9):
            c = row_twist[k - 1 : k, :]
            s = row_twist[k + 7 : k + 8, :]
            to = pl.ds(pl.multiple_of(64 * (k - 1) + 8 * g, 8), 8)
            gr, gi = abuf[to, 0:128], abuf[to, 128:256]
            re[k] = gr * c + gi * s
            if k < 8:
                im[k] = gi * c - gr * s
        re[0] = abuf[pl.ds(pl.multiple_of(512 + 8 * g, 8), 8), 0:128]
        cosine = cosine_16(re[0], re[8], re)
        sine = sine_16(im)
        at = pl.ds(pl.multiple_of(8 * g, 8), 8)
        edges = {}
        for a in range(16):
            if a == 0 or a == 8:
                blurred = cosine[a]
            elif a < 8:
                blurred = cosine[a] - sine[a]
            else:
                blurred = cosine[16 - a] + sine[16 - a]
            lanes = slice(128 * a, 128 * a + 128)
            blur_ref[at, lanes] = blurred
            halfway = est[at, lanes] + step_size * (dirty[at, lanes] - blurred)
            hz[a // 4, at, 128 * (a % 4) : 128 * (a % 4) + 128] = halfway
            if a % 4 in (0, 3):
                edges[a] = halfway
        for c in range(Z):
            right = edges[4 * c + 4] if c < Z - 1 else jnp.zeros((8, 128), F32)
            left = edges[4 * c - 1] if c > 0 else jnp.zeros((8, 128), F32)
            hh[c, at, :] = roll(jnp.where(left_lanes, right, left), 16, 1)
        return carry

    lax.fori_loop(0, 8, rows_inverse, 0)

    lane_group = lax.broadcasted_iota(jnp.int32, (16, 128), 1) // 32
    for c in range(Z):
        packed = hh[c, 0:16, :]
        for g in range(1, 4):
            packed = jnp.where(lane_group == g, roll(hh[c, 16 * g : 16 * g + 16, :], 32 * g, 1), packed)
        hp[c] = packed

    def copy_p(to, slot, sem):
        return pltpu.make_async_remote_copy(
            src_ref=hp.at[to],
            dst_ref=hpr.at[slot],
            send_sem=p_send.at[to],
            recv_sem=p_recv.at[sem],
            device_id={"chan": to},
            device_id_type=MESH,
        )

    def copy_z(to, slot, sem):
        return pltpu.make_async_remote_copy(
            src_ref=hz.at[to],
            dst_ref=hr.at[slot, 16:80, 0:512],
            send_sem=z_send.at[to],
            recv_sem=z_recv.at[sem],
            device_id={"chan": to},
            device_id_type=MESH,
        )

    for i in range(1, Z):
        copy_p(lax.rem(z + i, Z), z, z).start()
        copy_z(lax.rem(z + i, Z), z, z).start()
    own3 = pltpu.make_async_copy(hz.at[z], hr.at[z, 16:80, 0:512], own_sem)
    own3.start()
    hpr[z] = hp[z]

    @pl.when(p == 0)
    def _():
        hr[:, 0:16, :] = jnp.zeros((Z, 16, 640), F32)

    @pl.when(p == R - 1)
    def _():
        hr[:, 80:96, :] = jnp.zeros((Z, 16, 640), F32)

    for i in range(1, Z):
        other = lax.rem(z + Z - i, Z)
        copy_p(other, other, other).wait_recv()
        copy_z(other, other, other).wait_recv()
    own3.wait()
    for i in range(1, Z):
        copy_p(lax.rem(z + i, Z), z, z).wait_send()
        copy_z(lax.rem(z + i, Z), z, z).wait_send()
    for c in range(Z):
        for g in range(4):
            hr[c, 16 + 16 * g : 32 + 16 * g, 512:640] = roll(hpr[c], -32 * g - 16, 1)

    above = pltpu.make_async_remote_copy(
        src_ref=hr.at[:, 16:32, :],
        dst_ref=hr.at[:, 80:96, :],
        send_sem=h_send.at[0],
        recv_sem=h_recv.at[0],
        device_id={"rows": lax.rem(p + R - 1, R)},
        device_id_type=MESH,
    )
    below = pltpu.make_async_remote_copy(
        src_ref=hr.at[:, 64:80, :],
        dst_ref=hr.at[:, 0:16, :],
        send_sem=h_send.at[1],
        recv_sem=h_recv.at[1],
        device_id={"rows": lax.rem(p + 1, R)},
        device_id_type=MESH,
    )

    @pl.when(p > 0)
    def _():
        above.start()

    @pl.when(p < R - 1)
    def _():
        below.start()

    @pl.when(p < R - 1)
    def _():
        above.wait_recv()

    @pl.when(p > 0)
    def _():
        below.wait_recv()
        above.wait_send()

    @pl.when(p < R - 1)
    def _():
        below.wait_send()


    row_ids = lax.broadcasted_iota(jnp.int32, (96, 1), 0) + 64 * p - 16
    row_mask = jnp.logical_and(row_ids >= 0, row_ids < 64 * R).astype(F32)
    col_ids = lax.broadcasted_iota(jnp.int32, (1, 640), 1)
    right_zero = jnp.logical_and(z == Z - 1, jnp.logical_and(col_ids >= 512, col_ids < 576))
    left_zero = jnp.logical_and(z == 0, col_ids >= 576)
    col_mask = 1.0 - jnp.logical_or(right_zero, left_zero).astype(F32)

    def starlet(ch, carry):
        current = hr[ch]
        for level in range(3):
            later = smooth(current, 1 << level)
            if level < 2:
                later = later * row_mask * col_mask
            detail = (current - later)[16:80, 0:512]
            det[level, ch] = detail
            squared = detail * detail
            energy[level] = jnp.where(ch == 0, squared, energy[level] + squared)
            current = later
        return carry

    energy[...] = jnp.zeros((3, 64, 512), F32)
    lax.fori_loop(0, Z, starlet, 0)

    lane = lax.broadcasted_iota(jnp.int32, (1, 128), 1)
    peaks = jnp.zeros((1, 128), F32)
    for level in range(3):
        peaks = jnp.where(lane == level, jnp.max(energy[level]), peaks)
    mx_own[0] = peaks

    def copy_mz(to, slot):
        return pltpu.make_async_remote_copy(
            src_ref=mx_own.at[0],
            dst_ref=mx_z.at[slot],
            send_sem=mz_send.at[to],
            recv_sem=mz_recv.at[slot],
            device_id={"chan": to},
            device_id_type=MESH,
        )

    for i in range(1, Z):
        copy_mz(lax.rem(z + i, Z), z).start()
    mx_z[z] = peaks
    for i in range(1, Z):
        other = lax.rem(z + Z - i, Z)
        copy_mz(other, other).wait_recv()
    peaks = jnp.max(mx_z[...], axis=0)
    mx_own[1] = peaks

    def copy_mr(to, slot):
        return pltpu.make_async_remote_copy(
            src_ref=mx_own.at[1],
            dst_ref=mx_r.at[slot],
            send_sem=mr_send.at[to],
            recv_sem=mr_recv.at[slot],
            device_id={"rows": to},
            device_id_type=MESH,
        )

    def begin_mr(i, carry):
        copy_mr(lax.rem(p + i, R), p).start()
        return carry

    lax.fori_loop(1, R, begin_mr, 0)
    mx_r[p] = peaks
    energy[...] = lax.rsqrt(energy[...])

    def end_mr(i, carry):
        other = lax.rem(p + R - i, R)
        copy_mr(other, other).wait_recv()
        return carry

    lax.fori_loop(1, R, end_mr, 0)
    peaks = jnp.sqrt(jnp.max(mx_r[...], axis=0))
    thresholds = [
        fractions[level] * jnp.max(jnp.where(lane == level, peaks, 0.0)) for level in range(3)
    ]
    for level in range(3):
        energy[level] = jnp.minimum(energy[level] * thresholds[level], 1.0)

    def copy_o(to, slot, sem):
        return pltpu.make_async_remote_copy(
            src_ref=ob.at[to],
            dst_ref=shrink_ref.at[:, pl.ds(pl.multiple_of(512 * slot, 512), 512)],
            send_sem=o_send.at[to],
            recv_sem=o_recv.at[sem],
            device_id={"chan": to},
            device_id_type=MESH,
        )

    def shrunk(ch):
        out = energy[0] * det[0, ch]
        out = out + energy[1] * det[1, ch]
        return out + energy[2] * det[2, ch]

    def final(i, carry):
        ch = lax.rem(z + i, Z)
        ob[ch] = shrunk(ch)
        copy_o(ch, z, z).start()
        return carry

    lax.fori_loop(1, Z, final, 0)
    shrink_ref[:, pl.ds(pl.multiple_of(512 * z, 512), 512)] = shrunk(z)

    def sent3(i, carry):
        copy_mr(lax.rem(p + i, R), p).wait_send()
        return carry

    lax.fori_loop(1, R, sent3, 0)

    for i in range(1, Z):
        other = lax.rem(z + Z - i, Z)
        copy_o(other, other, other).wait_recv()
    for i in range(1, Z):
        to = lax.rem(z + i, Z)
        copy_mz(to, z).wait_send()
        copy_o(to, z, z).wait_send()


def shards(estimate, dirty_image, psf_weights):
    constants = tables()
    vmem = pl.BlockSpec(memory_space=pltpu.VMEM)
    block = jax.ShapeDtypeStruct((64, 2048), F32)
    dma = pltpu.SemaphoreType.DMA
    shrink, blurred = pl.pallas_call(
        kernel,
        out_shape=(block, block),
        in_specs=[vmem] * 9,
        out_specs=(vmem, vmem),
        scratch_shapes=[
            pltpu.VMEM((640, 256), F32),
            pltpu.VMEM((R, TILES, 8, 128), F32),
            pltpu.VMEM((R, TILES + 1, 8, 128), F32),
            pltpu.VMEM((256, 256), F32),
            pltpu.VMEM((R, TILES + 1, 8, 128), F32),
            pltpu.VMEM((R, TILES, 8, 128), F32),
            pltpu.VMEM((Z, 64, 512), F32),
            pltpu.VMEM((Z, 64, 128), F32),
            pltpu.VMEM((Z, 16, 128), F32),
            pltpu.VMEM((Z, 16, 128), F32),
            pltpu.VMEM((Z, 96, 640), F32),
            pltpu.VMEM((3, Z, 64, 512), F32),
            pltpu.VMEM((3, 64, 512), F32),
            pltpu.VMEM((Z, 64, 512), F32),
            pltpu.VMEM((2, 1, 128), F32),
            pltpu.VMEM((Z, 1, 128), F32),
            pltpu.VMEM((R, 1, 128), F32),
            pltpu.VMEM((3, 32, 8, 128), F32),
            pltpu.VMEM((2, 32, 8, 128), F32),
            pltpu.VMEM((2, 32, 8, 128), F32),
            pltpu.VMEM((2, 32, 8, 128), F32),
            dma, dma, dma((Z,)), dma((Z,)),
            dma((R,)), dma((R,)), dma((R,)), dma((R,)),
            dma((Z,)), dma((Z,)), dma((2,)), dma((2,)), dma((Z,)), dma((Z,)),
            dma((Z,)), dma((Z,)), dma((R,)), dma((R,)), dma,
        ],
        compiler_params=pltpu.CompilerParams(collective_id=0, has_side_effects=True),
    )(estimate[0], dirty_image[0], psf_weights[0], *constants)
    residual = dirty_image[0] - blurred
    new = estimate[0] + step_size * residual - shrink
    return (new[None], residual[None])


def solution(mesh):
    return jax.shard_map(
        shards,
        mesh=mesh,
        in_specs=(P("chan", "rows", None), P("chan", "rows", None), P("chan", None, "rows")),
        out_specs=(P("chan", "rows", None), P("chan", "rows", None)),
        check_vma=False,
    )
```

```python
import functools
import math

import jax
import jax.numpy as jnp
import numpy as np
from jax import lax
from jax.experimental import pallas as pl
from jax.experimental.pallas import tpu as pltpu
from jax.sharding import PartitionSpec as P

fractions = (0.03, 0.02, 0.015)
step_size = 0.9
MESH = pl.DeviceIdType.MESH
F32 = jnp.float32
BF16 = jnp.bfloat16
R = 32
Z = 4
VMEM_LIMIT = 60 * 1024 * 1024
TILES = 5


def linear(pairs):
    total = None
    for coef, value in pairs:
        if abs(coef) < 1e-12:
            continue
        if abs(coef - 1.0) < 1e-12:
            total = value if total is None else total + value
        elif abs(coef + 1.0) < 1e-12:
            total = -value if total is None else total - value
        else:
            term = coef * value
            total = term if total is None else total + term
    return total


def cosine_16(first, middle, e):
    out = [None] * 9
    for k in range(5):
        even = linear(
            [(1.0, first), (1.0 if k % 2 == 0 else -1.0, middle)]
            + [(math.cos(2 * math.pi * k * a / 16), e[a]) for a in (2, 4, 6)]
        )
        odd = linear([(math.cos(2 * math.pi * k * a / 16), e[a]) for a in (1, 3, 5, 7)])
        if odd is None:
            out[k] = even
            out[8 - k] = even
        else:
            out[k] = even + odd
            out[8 - k] = even - odd
    return out


def sine_16(o):
    out = [None] * 8
    for k in range(1, 5):
        even = linear([(math.sin(2 * math.pi * k * a / 16), o[a]) for a in (2, 4, 6)])
        odd = linear([(math.sin(2 * math.pi * k * a / 16), o[a]) for a in (1, 3, 5, 7)])
        if even is None:
            out[k] = odd
        else:
            out[k] = odd + even
            out[8 - k] = odd - even
    return out


def fft(values, sign):
    count = len(values)
    if count == 1:
        return values
    if count == 2:
        (ar, ai), (br, bi) = values
        return [(ar + br, ai + bi), (ar - br, ai - bi)]
    if count == 4:
        (ar, ai), (br, bi), (cr, ci), (dr, di) = values
        sr, si, tr, ti = ar + cr, ai + ci, ar - cr, ai - ci
        ur, ui, vr, vi = br + dr, bi + di, br - dr, bi - di
        if sign > 0:
            return [(sr + ur, si + ui), (tr - vi, ti + vr), (sr - ur, si - ui), (tr + vi, ti - vr)]
        return [(sr + ur, si + ui), (tr + vi, ti - vr), (sr - ur, si - ui), (tr - vi, ti + vr)]
    quarter = count // 4
    parts = [fft(values[n::4], sign) for n in range(4)]
    out = [None] * count
    for k in range(quarter):
        four = []
        for n in range(4):
            re, im = parts[n][k]
            angle = sign * 2 * math.pi * n * k / count
            c, s = math.cos(angle), math.sin(angle)
            if n * k == 0:
                four.append((re, im))
            elif abs(abs(c) - abs(s)) < 1e-9:
                h = abs(c)
                cs, ss = math.copysign(1, c), math.copysign(1, s)
                r = (re if cs > 0 else -re) - (im if ss > 0 else -im)
                i = (im if cs > 0 else -im) + (re if ss > 0 else -re)
                four.append((h * r, h * i))
            else:
                four.append((re * c - im * s, re * s + im * c))
        for m, value in enumerate(fft(four, sign)):
            out[k + m * quarter] = value
    return out


def split(value):
    high = value.astype(BF16)
    return high, (value - high.astype(F32)).astype(BF16)


def dot3(a, b, dims):
    (ah, al), (bh, bl) = a, b
    dot = functools.partial(
        lax.dot_general, dimension_numbers=(dims, ((), ())), preferred_element_type=F32
    )
    return dot(ah, bh) + (dot(al, bh) + dot(ah, bl))


def tables():
    m = np.arange(128)
    rows = np.zeros((256, 256))
    for d in range(32):
        for jj in range(4):
            angle = 2 * np.pi * ((4 * d + jj) * m % 128) / 128
            rows[8 * d + jj] = np.concatenate([np.cos(angle), np.sin(angle)])
            rows[8 * d + 4 + jj] = np.concatenate([-np.sin(angle), np.cos(angle)])
    n = np.arange(64)
    angle = 2 * np.pi * (n[:, None] * n[None, :] % 64) / 64
    cols = np.zeros((2, 2, 64, 2, 2, 64))
    for kk in range(2):
        cols[0, kk, :, 0, kk] = np.cos(angle)
        cols[1, kk, :, 0, kk] = np.sin(angle)
        cols[0, kk, :, 1, kk] = -np.sin(angle)
        cols[1, kk, :, 1, kk] = np.cos(angle)
    cols = cols.reshape(256, 256)
    early = np.concatenate([np.arange(16), np.arange(48, 64)])
    chunk = np.concatenate([early, np.arange(16, 48)]).reshape(2, 32)
    back = cols.T.reshape(256, 2, 2, 64)[:, :, :, chunk]
    back = back.transpose(0, 1, 3, 2, 4).reshape(256, 256)
    k = np.arange(1, 9)
    angle = -2 * np.pi * k[:, None] * m[None, :] / 2048
    row_twist = np.concatenate([np.cos(angle), np.sin(angle)])
    u1 = np.arange(32)
    angle = -2 * np.pi * u1[:, None] * n[None, :] / 2048
    angle = np.concatenate([angle, angle], axis=1)
    lanes = np.broadcast_to(chunk[:, None, :], (2, 2, 32)).reshape(128)
    turned = -2 * np.pi * u1[:, None] * lanes[None, :] / 2048
    col_twist = np.stack([np.cos(angle), np.sin(angle), np.cos(turned), np.sin(turned)])

    flip = np.zeros((2, 2, 128, 128))
    for kk in range(2):
        for u in range(64):
            flip[0, :, 64 * kk + 63 - u, 64 * kk + u] = 1.0
            flip[1, :, 64 * kk + (64 - u) % 64, 64 * kk + u] = 1.0
    pick = np.zeros((2, 40, 2, 64))
    for kk in range(2):
        for q in range(3):
            for half in range(2):
                s = 4 * q + 2 * half + kk
                k = s + 1 if s < 8 else 0
                for jj in range(4):
                    if s < 9:
                        pick[kk, 8 * q + 4 * half + jj, :, 16 * jj + k] = 2.0**-22
                    if s < 7:
                        pick[kk, 24 + 8 * q + 4 * half + jj, :, 16 * (3 - jj) + 16 - k] = 2.0**-22
    perm = np.concatenate([flip.reshape(512, 128), pick.reshape(80, 128)]).astype(BF16)

    def halves(table):
        high = table.astype(BF16)
        return np.stack([high, (table - high.astype(np.float64)).astype(BF16)])

    return (
        halves(rows),
        halves(cols),
        halves(back),
        np.asarray(row_twist, np.float32),
        np.asarray(col_twist, np.float32),
        perm,
    )


def roll(value, shift, axis):
    return pltpu.roll(value, shift % value.shape[axis], axis)


def smooth(value, spacing):
    for axis in (1, 0):
        value = value + roll(value, spacing, axis)
        value = value + roll(value, -spacing, axis)
        value = value + roll(value, spacing, axis)
        value = value + roll(value, -spacing, axis)
    return value * (1.0 / 256.0)


def drain(ref, sem):
    pltpu.make_async_copy(ref, ref, sem).wait()


def kernel(
    est_in, dirty_in, psf_in, row_table_in, col_table_in, col_back_in, row_twist_in, col_twist_in,
    perm_in,
    shrink_ref, blur_ref,
    est, dirty, psf_wide, row_table, col_table, col_back, row_twist, col_twist, perm,
    psf, abuf, send, recv, spec, send_a, send_b, recv_a, recv_b,
    hz, hh, hp, hpr, hr, det, energy, ob, mx_own, mx_z, mx_r,
    weights, mirror, flipped, mirror_in, in_sems, sems,
):
    z = lax.axis_index("chan")
    p = lax.axis_index("rows")

    barrier = pltpu.get_barrier_semaphore()

    def greet_row(i, carry):
        pl.semaphore_signal(
            barrier, inc=1, device_id={"rows": lax.rem(p + i, R)}, device_id_type=MESH
        )
        return carry

    def greet_chan(i, carry):
        pl.semaphore_signal(
            barrier, inc=1, device_id={"chan": lax.rem(z + i, Z)}, device_id_type=MESH
        )
        return carry

    lax.fori_loop(1, R, greet_row, 0)
    lax.fori_loop(1, Z, greet_chan, 0)

    pairs = (
        (est_in, est), (row_twist_in, row_twist), (row_table_in, row_table), (psf_in, psf_wide),
        (perm_in, perm), (col_twist_in, col_twist), (col_table_in, col_table),
        (col_back_in, col_back), (dirty_in, dirty),
    )
    loads = [pltpu.make_async_copy(a, b, in_sems.at[i]) for i, (a, b) in enumerate(pairs)]
    for load in loads:
        load.start()

    def remote(source, target, send_sem, recv_sem, **device):
        return pltpu.make_async_remote_copy(
            src_ref=source,
            dst_ref=target,
            send_sem=sems.at[send_sem],
            recv_sem=sems.at[recv_sem],
            device_id=device,
            device_id_type=MESH,
        )

    abuf[576:640, :] = jnp.zeros((64, 256), F32)
    for load in loads[:3]:
        load.wait()

    def rows_forward(g, carry):
        at = pl.ds(pl.multiple_of(8 * g, 8), 8)
        x = [est[at, 128 * a : 128 * a + 128] for a in range(16)]
        e = [None] + [x[a] + x[16 - a] for a in range(1, 8)]
        o = [None] + [x[a] - x[16 - a] for a in range(1, 8)]
        re = cosine_16(x[0], x[8], e)
        im = sine_16(o)
        for k in range(1, 9):
            c = row_twist[k - 1 : k, :]
            s = row_twist[k + 7 : k + 8, :]
            to = pl.ds(pl.multiple_of(64 * (k - 1) + 8 * g, 8), 8)
            if k < 8:
                abuf[to, 0:128] = re[k] * c + im[k] * s
                abuf[to, 128:256] = re[k] * s - im[k] * c
            else:
                abuf[to, 0:128] = re[k] * c
                abuf[to, 128:256] = re[k] * s
        to = pl.ds(pl.multiple_of(512 + 8 * g, 8), 8)
        abuf[to, 0:128] = re[0]
        abuf[to, 128:256] = jnp.zeros((8, 128), F32)
        return carry

    lax.fori_loop(0, 8, rows_forward, 0)
    table = (row_table[0], row_table[1])
    for t in range(TILES):
        out = dot3(table, split(abuf[128 * t : 128 * t + 128, :]), ((1,), (1,)))
        send[:, t] = out.reshape(R, 8, 128)

    left_half = lax.broadcasted_iota(jnp.int32, (40, 128), 1) < 64
    for load in loads[3:5]:
        load.wait()
    for b in range(16):
        psf[128 * b : 128 * b + 128, :] = jnp.transpose(psf_wide[:, 128 * b : 128 * b + 128])
    for i in range(8):
        rows = [psf[pl.ds(4 * i + n, 64, stride=32), :] for n in range(4)]
        high, low = split(jnp.concatenate(rows, axis=0))
        both = jnp.concatenate([high, low], axis=1)
        out = lax.dot_general(
            perm[512:592], both, (((1,), (1,)), ((), ())), preferred_element_type=F32
        )
        for n in range(2):
            a = out[0:40, 128 * n : 128 * n + 128]
            b = out[40:80, 128 * n : 128 * n + 128]
            first = jnp.where(left_half, a, roll(b, 64, 1))
            second = jnp.where(left_half, roll(a, 64, 1), b)
            for u1, value in ((4 * i + 2 * n, first), (4 * i + 2 * n + 1, second)):
                for q in range(3):
                    weights[q, u1] = value[8 * q : 8 * q + 8]
                for q in range(2):
                    mirror[q, u1] = value[24 + 8 * q : 32 + 8 * q]
    for q in range(2):
        high, low = split(mirror[q].reshape(256, 128))
        both = jnp.concatenate([high, low], axis=1)
        out = jnp.dot(both, perm[0:256], preferred_element_type=F32)
        zero = jnp.dot(both[0:16], perm[256:512], preferred_element_type=F32)
        flipped[q, 0] = zero[0:8]
        for u1 in range(1, 32):
            flipped[q, 32 - u1] = out[8 * u1 : 8 * u1 + 8]

    pl.semaphore_wait(barrier, R - 1 + Z - 1)

    partner = remote(flipped, mirror_in, 0, 1, rows=R - 1 - p)
    partner.start()

    def begin(i, carry):
        to = lax.rem(p + i, R)
        remote(send.at[to], recv.at[p, 0:TILES], 2, 3, rows=to).start()
        return carry

    lax.fori_loop(1, R, begin, 0)
    recv[p, 0:TILES] = send[p]
    recv[:, TILES] = jnp.zeros((R, 8, 128), F32)
    for load in loads[5:]:
        load.wait()
    drain(recv.at[0 : R - 1, 0:TILES], sems.at[3])
    drain(send.at[0 : R - 1], sems.at[2])
    partner.wait_recv()
    partner.wait_send()
    for q in range(2):
        weights[q] = weights[q] + mirror_in[q]

    upper = lax.broadcasted_iota(jnp.int32, (8, 128), 0) < 4
    left = lax.broadcasted_iota(jnp.int32, (8, 128), 1) < 64

    def columns(q, carry):
        values = []
        for i in range(R):
            a = recv[i, 2 * q]
            b = recv[i, 2 * q + 1]
            values.append(
                (jnp.where(upper, a, roll(b, 4, 0)), jnp.where(upper, roll(a, 4, 0), b))
            )
        for u, (re, im) in enumerate(fft(values, -1)):
            c = col_twist[0, u : u + 1, :]
            s = col_twist[1, u : u + 1, :]
            spec[8 * u : 8 * u + 8, 0:128] = re * c - im * s
            spec[8 * u : 8 * u + 8, 128:256] = re * s + im * c
        out = dot3(split(spec[...]), (col_table[0], col_table[1]), ((1,), (0,)))
        w = weights[q].reshape(256, 128)
        out = jnp.concatenate([out[:, 0:128] * w, out[:, 128:256] * w], axis=1)
        spec[...] = dot3(split(out), (col_back[0], col_back[1]), ((1,), (0,)))
        values = []
        for u in range(R):
            c = col_twist[2, u : u + 1, :]
            s = col_twist[3, u : u + 1, :]
            re = spec[8 * u : 8 * u + 8, 0:128]
            im = spec[8 * u : 8 * u + 8, 128:256]
            values.append((re * c + im * s, im * c - re * s))
        whole = jnp.logical_or(left, q == 2)
        for i, (re, im) in enumerate(fft(values, 1)):
            a = jnp.where(upper, re, roll(im, 4, 0))
            b = jnp.where(upper, roll(re, 4, 0), im)
            send_a[i, q] = jnp.where(whole, a, roll(b, 64, 1))
            send_b[i, q] = jnp.where(left, roll(a, 64, 1), b)
        return carry

    lax.fori_loop(0, 3, columns, 0)

    def begin_a(i, carry):
        to = lax.rem(p + i, R)
        remote(send_a.at[to], recv_a.at[p], 4, 5, rows=to).start()
        return carry

    def begin_b(i, carry):
        to = lax.rem(p + i, R)
        remote(send_b.at[to, 0:2], recv_b.at[p], 6, 7, rows=to).start()
        return carry

    lax.fori_loop(1, R, begin_a, 0)
    lax.fori_loop(1, R, begin_b, 0)
    recv_a[p] = send_a[p]
    recv_b[p] = send_b[p, 0:2]

    def rows_inverse(base, spread, first, last):
        def group(g, carry):
            re, im = [None] * 9, [None] * 8
            for k in range(1, 9):
                c = row_twist[k - 1 : k, :]
                s = row_twist[k + 7 : k + 8, :]
                to = pl.ds(pl.multiple_of(base + 32 * (k - 1) + 8 * g, 8), 8)
                gr, gi = abuf[to, 0:128], abuf[to, 128:256]
                re[k] = gr * c + gi * s
                if k < 8:
                    im[k] = gi * c - gr * s
            re[0] = abuf[pl.ds(pl.multiple_of(last + 8 * g, 8), 8), 0:128]
            cosine = cosine_16(re[0], re[8], re)
            sine = sine_16(im)
            at = pl.ds(pl.multiple_of(first + 8 * g + spread * (g // 2), 8), 8)
            edges = {}
            for a in range(16):
                if a == 0 or a == 8:
                    blurred = cosine[a]
                elif a < 8:
                    blurred = cosine[a] - sine[a]
                else:
                    blurred = cosine[16 - a] + sine[16 - a]
                lanes = slice(128 * a, 128 * a + 128)
                blur_ref[at, lanes] = blurred
                halfway = est[at, lanes] + step_size * (dirty[at, lanes] - blurred)
                hz[a // 4, at, 128 * (a % 4) : 128 * (a % 4) + 128] = halfway
                if a % 4 in (0, 3):
                    edges[a] = halfway
            none = jnp.zeros((8, 128), F32)
            for c in range(Z):
                after = edges[4 * c + 4] if c < Z - 1 else none
                before = edges[4 * c - 1] if c > 0 else none
                hh[c, at, :] = roll(jnp.where(left, after, before), 16, 1)
            return carry

        lax.fori_loop(0, 4, group, 0)

    lane_16 = lax.broadcasted_iota(jnp.int32, (16, 128), 1)

    def pack(half, groups):
        for c in range(Z):
            a, b = (hh[c, 16 * g : 16 * g + 16, :] for g in groups)
            hp[half, c] = jnp.where(lane_16 < 32, a, roll(b, 32, 1))

    def unpack(half, groups):
        for c in range(Z):
            for e, g in enumerate(groups):
                hr[c, 16 + 16 * g : 32 + 16 * g, 512:640] = roll(hpr[half, c], -32 * e - 16, 1)

    drain(recv_a.at[0 : R - 1], sems.at[5])
    for t in range(3):
        block = recv_a[:, t].reshape(256, 128)
        abuf[128 * t : 128 * t + 128, :] = dot3(split(block), table, ((0,), (0,)))
    rows_inverse(0, 32, 0, 256)
    pack(0, (0, 3))
    for i in range(1, Z):
        to = lax.rem(z + i, Z)
        for r in (0, 48):
            rows = slice(r, r + 16)
            remote(
                hz.at[to, rows], hr.at[z, r + 16 : r + 32, 0:512], 8, 9, chan=to
            ).start()
        remote(hp.at[0, to], hpr.at[0, z], 10, 11, chan=to).start()

    drain(recv_b.at[0 : R - 1], sems.at[7])
    for t in range(2):
        block = recv_b[:, t].reshape(256, 128)
        abuf[384 + 128 * t : 512 + 128 * t, :] = dot3(split(block), table, ((0,), (0,)))
    rows_inverse(384, 0, 16, 320)
    pack(1, (1, 2))
    for i in range(1, Z):
        to = lax.rem(z + i, Z)
        remote(hz.at[to, 16:48], hr.at[z, 32:64, 0:512], 12, 13, chan=to).start()
        remote(hp.at[1, to], hpr.at[1, z], 14, 15, chan=to).start()
    drain(send_a.at[0 : R - 1], sems.at[4])
    drain(send_b.at[0 : R - 1, 0:2], sems.at[6])
    hr[z, 16:80, 0:512] = hz[z]
    hpr[:, z] = hp[:, z]

    @pl.when(p == 0)
    def _():
        hr[:, 0:16, :] = jnp.zeros((Z, 16, 640), F32)

    @pl.when(p == R - 1)
    def _():
        hr[:, 80:96, :] = jnp.zeros((Z, 16, 640), F32)

    drain(hz.at[0 : Z - 1, 0:32], sems.at[9])
    drain(hp.at[0, 0 : Z - 1], sems.at[11])
    unpack(0, (0, 3))
    above = remote(hr.at[:, 16:32, :], hr.at[:, 80:96, :], 16, 17, rows=lax.rem(p + R - 1, R))
    below = remote(hr.at[:, 64:80, :], hr.at[:, 0:16, :], 18, 19, rows=lax.rem(p + 1, R))

    @pl.when(p > 0)
    def _():
        above.start()

    @pl.when(p < R - 1)
    def _():
        below.start()

    drain(hz.at[0 : Z - 1, 0:32], sems.at[13])
    drain(hp.at[0, 0 : Z - 1], sems.at[15])
    unpack(1, (1, 2))
    drain(hz.at[0 : Z - 1, 0:32], sems.at[8])
    drain(hp.at[0, 0 : Z - 1], sems.at[10])
    drain(hz.at[0 : Z - 1, 0:32], sems.at[12])
    drain(hp.at[0, 0 : Z - 1], sems.at[14])

    @pl.when(p < R - 1)
    def _():
        above.wait_recv()

    @pl.when(p > 0)
    def _():
        below.wait_recv()
        above.wait_send()

    @pl.when(p < R - 1)
    def _():
        below.wait_send()


    row_ids = lax.broadcasted_iota(jnp.int32, (96, 1), 0) + 64 * p - 16
    row_mask = jnp.logical_and(row_ids >= 0, row_ids < 64 * R).astype(F32)
    col_ids = lax.broadcasted_iota(jnp.int32, (1, 640), 1)
    right_zero = jnp.logical_and(z == Z - 1, jnp.logical_and(col_ids >= 512, col_ids < 576))
    left_zero = jnp.logical_and(z == 0, col_ids >= 576)
    col_mask = 1.0 - jnp.logical_or(right_zero, left_zero).astype(F32)

    def starlet(ch, carry):
        current = hr[ch]
        for level in range(3):
            later = smooth(current, 1 << level)
            if level < 2:
                later = later * row_mask * col_mask
            detail = (current - later)[16:80, 0:512]
            det[level, ch] = detail
            energy[level] = energy[level] + detail * detail
            current = later
        return carry

    energy[...] = jnp.zeros((3, 64, 512), F32)
    lax.fori_loop(0, Z, starlet, 0)

    lane = lax.broadcasted_iota(jnp.int32, (1, 128), 1)
    peaks = jnp.zeros((1, 128), F32)
    for level in range(3):
        peaks = jnp.where(lane == level, jnp.max(energy[level]), peaks)
    mx_own[0] = peaks
    for i in range(1, Z):
        remote(mx_own.at[0], mx_z.at[z], 20, 21, chan=lax.rem(z + i, Z)).start()
    mx_z[z] = peaks
    drain(mx_z.at[0 : Z - 1], sems.at[21])
    peaks = jnp.max(mx_z[...], axis=0)
    mx_own[1] = peaks

    def begin_max(i, carry):
        remote(mx_own.at[1], mx_r.at[p], 22, 23, rows=lax.rem(p + i, R)).start()
        return carry

    lax.fori_loop(1, R, begin_max, 0)
    mx_r[p] = peaks
    energy[...] = lax.rsqrt(energy[...])
    drain(mx_r.at[0 : R - 1], sems.at[23])
    drain(mx_r.at[0 : R - 1], sems.at[22])
    drain(mx_z.at[0 : Z - 1], sems.at[20])
    peaks = jnp.sqrt(jnp.max(mx_r[...], axis=0))
    for level in range(3):
        threshold = fractions[level] * jnp.max(jnp.where(lane == level, peaks, 0.0))
        energy[level] = jnp.minimum(energy[level] * threshold, 1.0)

    def shrunk(ch):
        out = energy[0] * det[0, ch]
        out = out + energy[1] * det[1, ch]
        return out + energy[2] * det[2, ch]

    block = pl.ds(pl.multiple_of(512 * z, 512), 512)

    def final(i, carry):
        ch = lax.rem(z + i, Z)
        ob[ch] = shrunk(ch)
        remote(ob.at[ch], shrink_ref.at[:, block], 24, 25, chan=ch).start()
        return carry

    lax.fori_loop(1, Z, final, 0)
    shrink_ref[:, block] = shrunk(z)
    drain(ob.at[0 : Z - 1], sems.at[25])
    drain(ob.at[0 : Z - 1], sems.at[24])


def shards(estimate, dirty_image, psf_weights):
    constants = tables()
    arguments = (estimate[0], dirty_image[0], psf_weights[0].T, *constants)
    anywhere = pl.BlockSpec(memory_space=pl.ANY)
    vmem = pl.BlockSpec(memory_space=pltpu.VMEM)
    block = jax.ShapeDtypeStruct((64, 2048), F32)
    dma = pltpu.SemaphoreType.DMA
    shapes = [
        (2048, 64),
        (640, 256),
        (R, TILES, 8, 128),
        (R, TILES + 1, 8, 128),
        (256, 256),
        (R, 3, 8, 128),
        (R, 3, 8, 128),
        (R, 3, 8, 128),
        (R, 2, 8, 128),
        (Z, 64, 512),
        (Z, 64, 128),
        (2, Z, 16, 128),
        (2, Z, 16, 128),
        (Z, 96, 640),
        (3, Z, 64, 512),
        (3, 64, 512),
        (Z, 64, 512),
        (2, 1, 128),
        (Z, 1, 128),
        (R, 1, 128),
        (3, 32, 8, 128),
        (2, 32, 8, 128),
        (2, 32, 8, 128),
        (2, 32, 8, 128),
    ]
    shrink, blurred = pl.pallas_call(
        kernel,
        out_shape=(block, block),
        in_specs=[anywhere] * len(arguments),
        out_specs=(vmem, vmem),
        scratch_shapes=[pltpu.VMEM(a.shape, a.dtype) for a in arguments]
        + [pltpu.VMEM(shape, F32) for shape in shapes]
        + [dma((len(arguments),)), dma((26,))],
        compiler_params=pltpu.CompilerParams(
            collective_id=0, has_side_effects=True, vmem_limit_bytes=VMEM_LIMIT
        ),
    )(*arguments)
    residual = dirty_image[0] - blurred
    new = estimate[0] + step_size * residual - shrink
    return (new[None], residual[None])


def solution(mesh):
    return jax.shard_map(
        shards,
        mesh=mesh,
        in_specs=(P("chan", "rows", None), P("chan", "rows", None), P("chan", None, "rows")),
        out_specs=(P("chan", "rows", None), P("chan", "rows", None)),
        check_vma=False,
    )
```

```python
import functools
import math

import jax
import jax.numpy as jnp
import numpy as np
from jax import lax
from jax.experimental import pallas as pl
from jax.experimental.pallas import tpu as pltpu
from jax.sharding import PartitionSpec as P

fractions = (0.03, 0.02, 0.015)
step_size = 0.9
MESH = pl.DeviceIdType.MESH
F32 = jnp.float32
BF16 = jnp.bfloat16
R = 32
Z = 4
VMEM_LIMIT = 60 * 1024 * 1024
TILES = 5


def linear(pairs):
    total = None
    for coef, value in pairs:
        if abs(coef) < 1e-12:
            continue
        if abs(coef - 1.0) < 1e-12:
            total = value if total is None else total + value
        elif abs(coef + 1.0) < 1e-12:
            total = -value if total is None else total - value
        else:
            term = coef * value
            total = term if total is None else total + term
    return total


def cosine_16(first, middle, e):
    out = [None] * 9
    for k in range(5):
        even = linear(
            [(1.0, first), (1.0 if k % 2 == 0 else -1.0, middle)]
            + [(math.cos(2 * math.pi * k * a / 16), e[a]) for a in (2, 4, 6)]
        )
        odd = linear([(math.cos(2 * math.pi * k * a / 16), e[a]) for a in (1, 3, 5, 7)])
        if odd is None:
            out[k] = even
            out[8 - k] = even
        else:
            out[k] = even + odd
            out[8 - k] = even - odd
    return out


def sine_16(o):
    out = [None] * 8
    for k in range(1, 5):
        even = linear([(math.sin(2 * math.pi * k * a / 16), o[a]) for a in (2, 4, 6)])
        odd = linear([(math.sin(2 * math.pi * k * a / 16), o[a]) for a in (1, 3, 5, 7)])
        if even is None:
            out[k] = odd
        else:
            out[k] = odd + even
            out[8 - k] = odd - even
    return out


def fft(values, sign):
    count = len(values)
    if count == 1:
        return values
    if count == 2:
        (ar, ai), (br, bi) = values
        return [(ar + br, ai + bi), (ar - br, ai - bi)]
    if count == 4:
        (ar, ai), (br, bi), (cr, ci), (dr, di) = values
        sr, si, tr, ti = ar + cr, ai + ci, ar - cr, ai - ci
        ur, ui, vr, vi = br + dr, bi + di, br - dr, bi - di
        if sign > 0:
            return [(sr + ur, si + ui), (tr - vi, ti + vr), (sr - ur, si - ui), (tr + vi, ti - vr)]
        return [(sr + ur, si + ui), (tr + vi, ti - vr), (sr - ur, si - ui), (tr - vi, ti + vr)]
    quarter = count // 4
    parts = [fft(values[n::4], sign) for n in range(4)]
    out = [None] * count
    for k in range(quarter):
        four = []
        for n in range(4):
            re, im = parts[n][k]
            angle = sign * 2 * math.pi * n * k / count
            c, s = math.cos(angle), math.sin(angle)
            if n * k == 0:
                four.append((re, im))
            elif abs(abs(c) - abs(s)) < 1e-9:
                h = abs(c)
                cs, ss = math.copysign(1, c), math.copysign(1, s)
                r = (re if cs > 0 else -re) - (im if ss > 0 else -im)
                i = (im if cs > 0 else -im) + (re if ss > 0 else -re)
                four.append((h * r, h * i))
            else:
                four.append((re * c - im * s, re * s + im * c))
        for m, value in enumerate(fft(four, sign)):
            out[k + m * quarter] = value
    return out


def split(value):
    high = value.astype(BF16)
    return high, (value - high.astype(F32)).astype(BF16)


def dot3(a, b, dims):
    (ah, al), (bh, bl) = a, b
    dot = functools.partial(
        lax.dot_general, dimension_numbers=(dims, ((), ())), preferred_element_type=F32
    )
    return dot(ah, bh) + (dot(al, bh) + dot(ah, bl))


def tables():
    m = np.arange(128)
    rows = np.zeros((256, 256))
    for d in range(32):
        for jj in range(4):
            angle = 2 * np.pi * ((4 * d + jj) * m % 128) / 128
            rows[8 * d + jj] = np.concatenate([np.cos(angle), np.sin(angle)])
            rows[8 * d + 4 + jj] = np.concatenate([-np.sin(angle), np.cos(angle)])
    n = np.arange(64)
    angle = 2 * np.pi * (n[:, None] * n[None, :] % 64) / 64
    cols = np.zeros((2, 2, 64, 2, 2, 64))
    for kk in range(2):
        cols[0, kk, :, 0, kk] = np.cos(angle)
        cols[1, kk, :, 0, kk] = np.sin(angle)
        cols[0, kk, :, 1, kk] = -np.sin(angle)
        cols[1, kk, :, 1, kk] = np.cos(angle)
    cols = cols.reshape(256, 256)
    early = np.concatenate([np.arange(16), np.arange(48, 64)])
    chunk = np.concatenate([early, np.arange(16, 48)]).reshape(2, 32)
    back = cols.T.reshape(256, 2, 2, 64)[:, :, :, chunk]
    back = back.transpose(0, 1, 3, 2, 4).reshape(256, 256)
    k = np.arange(1, 9)
    angle = -2 * np.pi * k[:, None] * m[None, :] / 2048
    row_twist = np.concatenate([np.cos(angle), np.sin(angle)])
    u1 = np.arange(32)
    angle = -2 * np.pi * u1[:, None] * n[None, :] / 2048
    angle = np.concatenate([angle, angle], axis=1)
    lanes = np.broadcast_to(chunk[:, None, :], (2, 2, 32)).reshape(128)
    turned = -2 * np.pi * u1[:, None] * lanes[None, :] / 2048
    col_twist = np.stack([np.cos(angle), np.sin(angle), np.cos(turned), np.sin(turned)])

    flip = np.zeros((2, 2, 128, 128))
    for kk in range(2):
        for u in range(64):
            flip[0, :, 64 * kk + 63 - u, 64 * kk + u] = 1.0
            flip[1, :, 64 * kk + (64 - u) % 64, 64 * kk + u] = 1.0
    pick = np.zeros((2, 40, 2, 64))
    for kk in range(2):
        for q in range(3):
            for half in range(2):
                s = 4 * q + 2 * half + kk
                k = s + 1 if s < 8 else 0
                for jj in range(4):
                    if s < 9:
                        pick[kk, 8 * q + 4 * half + jj, :, 16 * jj + k] = 2.0**-22
                    if s < 7:
                        pick[kk, 24 + 8 * q + 4 * half + jj, :, 16 * (3 - jj) + 16 - k] = 2.0**-22
    perm = np.concatenate([flip.reshape(512, 128), pick.reshape(80, 128)]).astype(BF16)

    def halves(table):
        high = table.astype(BF16)
        return np.stack([high, (table - high.astype(np.float64)).astype(BF16)])

    return (
        halves(rows),
        halves(cols),
        halves(back),
        np.asarray(row_twist, np.float32),
        np.asarray(col_twist, np.float32),
        perm,
    )


def roll(value, shift, axis):
    return pltpu.roll(value, shift % value.shape[axis], axis)


hops = ((2, 2), (1, 1), (3, 3), (1, 3), (3, 1), (2, 1), (1, 2), (2, 3))
hops = hops + ((3, 2), (2, 0), (0, 2), (1, 0), (0, 1), (3, 0), (0, 3), (0, 0))


def others(p):
    core, x, y = lax.rem(p, 2), lax.rem(p // 2, 4), p // 8
    for far in (0, 1):
        for dy, dx in hops:
            if (dy, dx, far) != (0, 0, 0):
                yield lax.rem(y + dy, 4) * 8 + lax.rem(x + dx, 4) * 2 + lax.rem(core + far, 2)


def drain(ref, sem):
    pltpu.make_async_copy(ref, ref, sem).wait()


def kernel(
    est_in, dirty_in, psf_in, row_table_in, col_table_in, col_back_in, row_twist_in, col_twist_in,
    perm_in,
    shrink_ref, blur_ref,
    est, dirty, psf_wide, row_table, col_table, col_back, row_twist, col_twist, perm,
    psf, abuf, send, recv, spec, send_a, send_b, recv_a, recv_b,
    hz, hh, hp, hpr, hr, rows_done, smooth_a, smooth_b, det, energy, ob, mx_own, mx_z, mx_r,
    weights, mirror, flipped, mirror_in, in_sems, sems,
):
    z = lax.axis_index("chan")
    p = lax.axis_index("rows")

    barrier = pltpu.get_barrier_semaphore()

    def greet_row(i, carry):
        pl.semaphore_signal(
            barrier, inc=1, device_id={"rows": lax.rem(p + i, R)}, device_id_type=MESH
        )
        return carry

    def greet_chan(i, carry):
        pl.semaphore_signal(
            barrier, inc=1, device_id={"chan": lax.rem(z + i, Z)}, device_id_type=MESH
        )
        return carry

    lax.fori_loop(1, R, greet_row, 0)
    lax.fori_loop(1, Z, greet_chan, 0)

    pairs = (
        (est_in, est), (row_twist_in, row_twist), (row_table_in, row_table), (psf_in, psf_wide),
        (perm_in, perm), (col_twist_in, col_twist), (col_table_in, col_table),
        (col_back_in, col_back), (dirty_in, dirty),
    )
    loads = [pltpu.make_async_copy(a, b, in_sems.at[i]) for i, (a, b) in enumerate(pairs)]
    for load in loads:
        load.start()

    def remote(source, target, send_sem, recv_sem, **device):
        return pltpu.make_async_remote_copy(
            src_ref=source,
            dst_ref=target,
            send_sem=sems.at[send_sem],
            recv_sem=sems.at[recv_sem],
            device_id=device,
            device_id_type=MESH,
        )

    abuf[576:640, :] = jnp.zeros((64, 256), F32)
    for load in loads[:3]:
        load.wait()

    def rows_forward(g, carry):
        at = pl.ds(pl.multiple_of(8 * g, 8), 8)
        x = [est[at, 128 * a : 128 * a + 128] for a in range(16)]
        e = [None] + [x[a] + x[16 - a] for a in range(1, 8)]
        o = [None] + [x[a] - x[16 - a] for a in range(1, 8)]
        re = cosine_16(x[0], x[8], e)
        im = sine_16(o)
        for k in range(1, 9):
            c = row_twist[k - 1 : k, :]
            s = row_twist[k + 7 : k + 8, :]
            to = pl.ds(pl.multiple_of(64 * (k - 1) + 8 * g, 8), 8)
            if k < 8:
                abuf[to, 0:128] = re[k] * c + im[k] * s
                abuf[to, 128:256] = re[k] * s - im[k] * c
            else:
                abuf[to, 0:128] = re[k] * c
                abuf[to, 128:256] = re[k] * s
        to = pl.ds(pl.multiple_of(512 + 8 * g, 8), 8)
        abuf[to, 0:128] = re[0]
        abuf[to, 128:256] = jnp.zeros((8, 128), F32)
        return carry

    lax.fori_loop(0, 8, rows_forward, 0)
    table = (row_table[0], row_table[1])
    for t in range(TILES):
        out = dot3(table, split(abuf[128 * t : 128 * t + 128, :]), ((1,), (1,)))
        send[:, t] = out.reshape(R, 8, 128)

    left_half = lax.broadcasted_iota(jnp.int32, (40, 128), 1) < 64
    for load in loads[3:5]:
        load.wait()
    for b in range(16):
        psf[128 * b : 128 * b + 128, :] = jnp.transpose(psf_wide[:, 128 * b : 128 * b + 128])
    for i in range(8):
        rows = [psf[pl.ds(4 * i + n, 64, stride=32), :] for n in range(4)]
        high, low = split(jnp.concatenate(rows, axis=0))
        both = jnp.concatenate([high, low], axis=1)
        out = lax.dot_general(
            perm[512:592], both, (((1,), (1,)), ((), ())), preferred_element_type=F32
        )
        for n in range(2):
            a = out[0:40, 128 * n : 128 * n + 128]
            b = out[40:80, 128 * n : 128 * n + 128]
            first = jnp.where(left_half, a, roll(b, 64, 1))
            second = jnp.where(left_half, roll(a, 64, 1), b)
            for u1, value in ((4 * i + 2 * n, first), (4 * i + 2 * n + 1, second)):
                for q in range(3):
                    weights[q, u1] = value[8 * q : 8 * q + 8]
                for q in range(2):
                    mirror[q, u1] = value[24 + 8 * q : 32 + 8 * q]
    for q in range(2):
        high, low = split(mirror[q].reshape(256, 128))
        both = jnp.concatenate([high, low], axis=1)
        out = jnp.dot(both, perm[0:256], preferred_element_type=F32)
        zero = jnp.dot(both[0:16], perm[256:512], preferred_element_type=F32)
        flipped[q, 0] = zero[0:8]
        for u1 in range(1, 32):
            flipped[q, 32 - u1] = out[8 * u1 : 8 * u1 + 8]

    pl.semaphore_wait(barrier, R - 1 + Z - 1)

    partner = remote(flipped, mirror_in, 0, 1, rows=R - 1 - p)
    partner.start()

    for to in others(p):
        remote(send.at[to], recv.at[p, 0:TILES], 2, 3, rows=to).start()
    recv[p, 0:TILES] = send[p]
    recv[:, TILES] = jnp.zeros((R, 8, 128), F32)
    for load in loads[5:]:
        load.wait()
    drain(recv.at[0 : R - 1, 0:TILES], sems.at[3])
    drain(send.at[0 : R - 1], sems.at[2])
    partner.wait_recv()
    partner.wait_send()
    for q in range(2):
        weights[q] = weights[q] + mirror_in[q]

    upper = lax.broadcasted_iota(jnp.int32, (8, 128), 0) < 4
    left = lax.broadcasted_iota(jnp.int32, (8, 128), 1) < 64

    def columns(q):
        values = []
        for i in range(R):
            a = recv[i, 2 * q]
            b = recv[i, 2 * q + 1]
            values.append(
                (jnp.where(upper, a, roll(b, 4, 0)), jnp.where(upper, roll(a, 4, 0), b))
            )
        for u, (re, im) in enumerate(fft(values, -1)):
            c = col_twist[0, u : u + 1, :]
            s = col_twist[1, u : u + 1, :]
            spec[8 * u : 8 * u + 8, 0:128] = re * c - im * s
            spec[8 * u : 8 * u + 8, 128:256] = re * s + im * c
        out = dot3(split(spec[...]), (col_table[0], col_table[1]), ((1,), (0,)))
        w = weights[q].reshape(256, 128)
        out = jnp.concatenate([out[:, 0:128] * w, out[:, 128:256] * w], axis=1)
        spec[...] = dot3(split(out), (col_back[0], col_back[1]), ((1,), (0,)))
        values = []
        for u in range(R):
            c = col_twist[2, u : u + 1, :]
            s = col_twist[3, u : u + 1, :]
            re = spec[8 * u : 8 * u + 8, 0:128]
            im = spec[8 * u : 8 * u + 8, 128:256]
            values.append((re * c + im * s, im * c - re * s))
        whole = jnp.logical_or(left, q == 2)
        for i, (re, im) in enumerate(fft(values, 1)):
            a = jnp.where(upper, re, roll(im, 4, 0))
            b = jnp.where(upper, roll(re, 4, 0), im)
            send_a[i, q] = jnp.where(whole, a, roll(b, 64, 1))
            send_b[i, q] = jnp.where(left, roll(a, 64, 1), b)

    def columns_and_send(q, carry):
        columns(q)
        for to in others(p):
            remote(send_a.at[to, q], recv_a.at[p, q], 4, 5, rows=to).start()
        return carry

    lax.fori_loop(0, 3, columns_and_send, 0)
    for to in others(p):
        remote(send_b.at[to, 0:2], recv_b.at[p], 6, 7, rows=to).start()
    recv_a[p] = send_a[p]
    recv_b[p] = send_b[p, 0:2]

    def rows_inverse(base, spread, first, last):
        def group(g, carry):
            re, im = [None] * 9, [None] * 8
            for k in range(1, 9):
                c = row_twist[k - 1 : k, :]
                s = row_twist[k + 7 : k + 8, :]
                to = pl.ds(pl.multiple_of(base + 32 * (k - 1) + 8 * g, 8), 8)
                gr, gi = abuf[to, 0:128], abuf[to, 128:256]
                re[k] = gr * c + gi * s
                if k < 8:
                    im[k] = gi * c - gr * s
            re[0] = abuf[pl.ds(pl.multiple_of(last + 8 * g, 8), 8), 0:128]
            cosine = cosine_16(re[0], re[8], re)
            sine = sine_16(im)
            at = pl.ds(pl.multiple_of(first + 8 * g + spread * (g // 2), 8), 8)
            edges = {}
            for a in range(16):
                if a == 0 or a == 8:
                    blurred = cosine[a]
                elif a < 8:
                    blurred = cosine[a] - sine[a]
                else:
                    blurred = cosine[16 - a] + sine[16 - a]
                lanes = slice(128 * a, 128 * a + 128)
                blur_ref[at, lanes] = blurred
                halfway = est[at, lanes] + step_size * (dirty[at, lanes] - blurred)
                hz[a // 4, at, 128 * (a % 4) : 128 * (a % 4) + 128] = halfway
                if a % 4 in (0, 3):
                    edges[a] = halfway
            none = jnp.zeros((8, 128), F32)
            for c in range(Z):
                after = edges[4 * c + 4] if c < Z - 1 else none
                before = edges[4 * c - 1] if c > 0 else none
                hh[c, at, :] = roll(jnp.where(left, after, before), 16, 1)
            return carry

        lax.fori_loop(0, 4, group, 0)

    lane_16 = lax.broadcasted_iota(jnp.int32, (16, 128), 1)

    def pack(half, groups):
        for c in range(Z):
            a, b = (hh[c, 16 * g : 16 * g + 16, :] for g in groups)
            hp[half, c] = jnp.where(lane_16 < 32, a, roll(b, 32, 1))

    def unpack(half, groups):
        for c in range(Z):
            for e, g in enumerate(groups):
                hr[c, 16 + 16 * g : 32 + 16 * g, 512:640] = roll(hpr[half, c], -32 * e - 16, 1)

    drain(recv_a.at[0 : R - 1], sems.at[5])
    for t in range(3):
        block = recv_a[:, t].reshape(256, 128)
        abuf[128 * t : 128 * t + 128, :] = dot3(split(block), table, ((0,), (0,)))
    rows_inverse(0, 32, 0, 256)
    pack(0, (0, 3))
    for i in (2, 1, 3):
        to = lax.rem(z + i, Z)
        for r in (0, 48):
            rows = slice(r, r + 16)
            remote(
                hz.at[to, rows], hr.at[z, r + 16 : r + 32, 0:512], 8, 9, chan=to
            ).start()
        remote(hp.at[0, to], hpr.at[0, z], 10, 11, chan=to).start()

    drain(recv_b.at[0 : R - 1], sems.at[7])
    for t in range(2):
        block = recv_b[:, t].reshape(256, 128)
        abuf[384 + 128 * t : 512 + 128 * t, :] = dot3(split(block), table, ((0,), (0,)))
    rows_inverse(384, 0, 16, 320)
    pack(1, (1, 2))
    for i in (2, 1, 3):
        to = lax.rem(z + i, Z)
        remote(hz.at[to, 16:48], hr.at[z, 32:64, 0:512], 12, 13, chan=to).start()
        remote(hp.at[1, to], hpr.at[1, z], 14, 15, chan=to).start()
    drain(send_a.at[0 : R - 1], sems.at[4])
    drain(send_b.at[0 : R - 1, 0:2], sems.at[6])
    hr[z, 16:80, 0:512] = hz[z]
    hpr[:, z] = hp[:, z]

    @pl.when(p == 0)
    def _():
        hr[:, 0:16, :] = jnp.zeros((Z, 16, 640), F32)

    @pl.when(p == R - 1)
    def _():
        hr[:, 80:96, :] = jnp.zeros((Z, 16, 640), F32)

    drain(hz.at[0 : Z - 1, 0:32], sems.at[9])
    drain(hp.at[0, 0 : Z - 1], sems.at[11])
    unpack(0, (0, 3))
    above = remote(hr.at[:, 16:32, :], hr.at[:, 80:96, :], 16, 17, rows=lax.rem(p + R - 1, R))
    below = remote(hr.at[:, 64:80, :], hr.at[:, 0:16, :], 18, 19, rows=lax.rem(p + 1, R))

    @pl.when(p > 0)
    def _():
        above.start()

    @pl.when(p < R - 1)
    def _():
        below.start()

    drain(hz.at[0 : Z - 1, 0:32], sems.at[13])
    drain(hp.at[0, 0 : Z - 1], sems.at[15])
    unpack(1, (1, 2))
    drain(hz.at[0 : Z - 1, 0:32], sems.at[8])
    drain(hp.at[0, 0 : Z - 1], sems.at[10])
    drain(hz.at[0 : Z - 1, 0:32], sems.at[12])
    drain(hp.at[0, 0 : Z - 1], sems.at[14])

    @pl.when(p < R - 1)
    def _():
        above.wait_recv()

    @pl.when(p > 0)
    def _():
        below.wait_recv()
        above.wait_send()

    @pl.when(p < R - 1)
    def _():
        below.wait_send()


    lane_8 = lax.broadcasted_iota(jnp.int32, (8, 128), 1)
    row_8 = lax.broadcasted_iota(jnp.int32, (8, 128), 0)
    top = jnp.where(p > 0, 1.0, 0.0)
    bottom = jnp.where(p < R - 1, 1.0, 0.0)
    side = jnp.where(
        lane_8 < 64, jnp.where(z < Z - 1, 1.0, 0.0), jnp.where(z > 0, 1.0, 0.0)
    )

    def down(x, spacing):
        count = len(x)
        if spacing == 4:
            turned = [roll(v, 4, 0) for v in x]
            mid = [None] + [
                jnp.where(row_8 < 4, turned[i - 1], turned[i]) for i in range(1, count)
            ]
            return [
                (x[i - 1] + x[i + 1]) * (1 / 256)
                + (x[i] * (6 / 256) + (mid[i] + mid[i + 1]) * (4 / 256))
                for i in range(1, count - 1)
            ]
        for step in range(4):
            if step % 2 == 0:
                turned = [roll(v, spacing, 0) for v in x]
                x = [x[0] + turned[0]] + [
                    x[i] + jnp.where(row_8 < spacing, turned[i - 1], turned[i])
                    for i in range(1, count)
                ]
            else:
                turned = [roll(v, -spacing, 0) for v in x]
                x = [
                    x[i] + jnp.where(row_8 >= 8 - spacing, turned[i + 1], turned[i])
                    for i in range(count - 1)
                ] + [x[-1] + turned[-1]]
        return [v * (1 / 256) for v in x]

    def along(x, spacing):
        for step in range(4):
            if step % 2 == 0:
                turned = [roll(v, spacing, 1) for v in x]
                x = [
                    x[t] + jnp.where(lane_8 < spacing, turned[t - 1], turned[t]) for t in range(5)
                ]
            else:
                turned = [roll(v, -spacing, 1) for v in x]
                x = [
                    x[t] + jnp.where(lane_8 >= 128 - spacing, turned[(t + 1) % 5], turned[t])
                    for t in range(5)
                ]
        return x

    def starlet(ch, carry):
        spans = ((0, 12, 0, 12), (0, 12, 1, 11), (1, 11, 2, 10))
        for level, (first, last, start, stop) in enumerate(spans):
            spacing = 1 << level
            source = (hr.at[ch], smooth_a, smooth_b)[level]
            target = (smooth_a, smooth_b, None)[level]
            for t in range(5):
                lanes = slice(128 * t, 128 * t + 128)
                x = [source[8 * i : 8 * i + 8, lanes] for i in range(first, last)]
                for i, value in enumerate(down(x, spacing)):
                    at = i + (first if spacing < 4 else first + 1)
                    if start <= at < stop:
                        rows_done[8 * at : 8 * at + 8, lanes] = value
            for i in range(start, stop):
                rows = slice(8 * i, 8 * i + 8)
                x = [rows_done[rows, 128 * t : 128 * t + 128] for t in range(5)]
                x = along(x, spacing)
                if target is not None:
                    if i < 2:
                        x = [v * top for v in x]
                    if i >= 10:
                        x = [v * bottom for v in x]
                    x[4] = x[4] * side
                    for t in range(5):
                        target[rows, 128 * t : 128 * t + 128] = x[t]
                if 2 <= i < 10:
                    at = slice(8 * i - 16, 8 * i - 8)
                    for t in range(4):
                        lanes = slice(128 * t, 128 * t + 128)
                        detail = source[rows, lanes] - x[t]
                        det[level, ch, at, lanes] = detail
                        energy[level, at, lanes] = energy[level, at, lanes] + detail * detail
        return carry

    energy[...] = jnp.zeros((3, 64, 512), F32)
    lax.fori_loop(0, Z, starlet, 0)

    lane = lax.broadcasted_iota(jnp.int32, (1, 128), 1)
    peaks = jnp.zeros((1, 128), F32)
    for level in range(3):
        peaks = jnp.where(lane == level, jnp.max(energy[level]), peaks)
    mx_own[0] = peaks
    for i in range(1, Z):
        remote(mx_own.at[0], mx_z.at[z], 20, 21, chan=lax.rem(z + i, Z)).start()
    mx_z[z] = peaks
    drain(mx_z.at[0 : Z - 1], sems.at[21])
    peaks = jnp.max(mx_z[...], axis=0)
    mx_own[1] = peaks

    def begin_max(i, carry):
        remote(mx_own.at[1], mx_r.at[p], 22, 23, rows=lax.rem(p + i, R)).start()
        return carry

    lax.fori_loop(1, R, begin_max, 0)
    mx_r[p] = peaks
    energy[...] = lax.rsqrt(energy[...])
    drain(mx_r.at[0 : R - 1], sems.at[23])
    drain(mx_r.at[0 : R - 1], sems.at[22])
    drain(mx_z.at[0 : Z - 1], sems.at[20])
    peaks = jnp.sqrt(jnp.max(mx_r[...], axis=0))
    for level in range(3):
        threshold = fractions[level] * jnp.max(jnp.where(lane == level, peaks, 0.0))
        energy[level] = jnp.minimum(energy[level] * threshold, 1.0)

    def shrunk(ch):
        out = energy[0] * det[0, ch]
        out = out + energy[1] * det[1, ch]
        return out + energy[2] * det[2, ch]

    block = pl.ds(pl.multiple_of(512 * z, 512), 512)

    def final(i, carry):
        ch = lax.rem(z + 2 - (i // 2) + 2 * (i // 3), Z)
        ob[ch] = shrunk(ch)
        remote(ob.at[ch], shrink_ref.at[:, block], 24, 25, chan=ch).start()
        return carry

    lax.fori_loop(1, Z, final, 0)
    shrink_ref[:, block] = shrunk(z)
    drain(ob.at[0 : Z - 1], sems.at[25])
    drain(ob.at[0 : Z - 1], sems.at[24])


def shards(estimate, dirty_image, psf_weights):
    constants = tables()
    arguments = (estimate[0], dirty_image[0], psf_weights[0].T, *constants)
    anywhere = pl.BlockSpec(memory_space=pl.ANY)
    vmem = pl.BlockSpec(memory_space=pltpu.VMEM)
    block = jax.ShapeDtypeStruct((64, 2048), F32)
    dma = pltpu.SemaphoreType.DMA
    shapes = [
        (2048, 64),
        (640, 256),
        (R, TILES, 8, 128),
        (R, TILES + 1, 8, 128),
        (256, 256),
        (R, 3, 8, 128),
        (R, 3, 8, 128),
        (R, 3, 8, 128),
        (R, 2, 8, 128),
        (Z, 64, 512),
        (Z, 64, 128),
        (2, Z, 16, 128),
        (2, Z, 16, 128),
        (Z, 96, 640),
        (96, 640),
        (96, 640),
        (96, 640),
        (3, Z, 64, 512),
        (3, 64, 512),
        (Z, 64, 512),
        (2, 1, 128),
        (Z, 1, 128),
        (R, 1, 128),
        (3, 32, 8, 128),
        (2, 32, 8, 128),
        (2, 32, 8, 128),
        (2, 32, 8, 128),
    ]
    shrink, blurred = pl.pallas_call(
        kernel,
        out_shape=(block, block),
        in_specs=[anywhere] * len(arguments),
        out_specs=(vmem, vmem),
        scratch_shapes=[pltpu.VMEM(a.shape, a.dtype) for a in arguments]
        + [pltpu.VMEM(shape, F32) for shape in shapes]
        + [dma((len(arguments),)), dma((26,))],
        compiler_params=pltpu.CompilerParams(
            collective_id=0, has_side_effects=True, vmem_limit_bytes=VMEM_LIMIT
        ),
    )(*arguments)
    residual = dirty_image[0] - blurred
    new = estimate[0] + step_size * residual - shrink
    return (new[None], residual[None])


def solution(mesh):
    return jax.shard_map(
        shards,
        mesh=mesh,
        in_specs=(P("chan", "rows", None), P("chan", "rows", None), P("chan", None, "rows")),
        out_specs=(P("chan", "rows", None), P("chan", "rows", None)),
        check_vma=False,
    )
```

```python
import functools
import math

import jax
import jax.numpy as jnp
import numpy as np
from jax import lax
from jax.experimental import pallas as pl
from jax.experimental.pallas import tpu as pltpu
from jax.sharding import PartitionSpec as P

fractions = (0.03, 0.02, 0.015)
step_size = 0.9
MESH = pl.DeviceIdType.MESH
F32 = jnp.float32
BF16 = jnp.bfloat16
R = 32
Z = 4
VMEM_LIMIT = 60 * 1024 * 1024
TILES = 5


def linear(pairs):
    total = None
    for coef, value in pairs:
        if abs(coef) < 1e-12:
            continue
        if abs(coef - 1.0) < 1e-12:
            total = value if total is None else total + value
        elif abs(coef + 1.0) < 1e-12:
            total = -value if total is None else total - value
        else:
            term = coef * value
            total = term if total is None else total + term
    return total


def cosine_16(first, middle, e):
    out = [None] * 9
    for k in range(5):
        even = linear(
            [(1.0, first), (1.0 if k % 2 == 0 else -1.0, middle)]
            + [(math.cos(2 * math.pi * k * a / 16), e[a]) for a in (2, 4, 6)]
        )
        odd = linear([(math.cos(2 * math.pi * k * a / 16), e[a]) for a in (1, 3, 5, 7)])
        if odd is None:
            out[k] = even
            out[8 - k] = even
        else:
            out[k] = even + odd
            out[8 - k] = even - odd
    return out


def sine_16(o):
    out = [None] * 8
    for k in range(1, 5):
        even = linear([(math.sin(2 * math.pi * k * a / 16), o[a]) for a in (2, 4, 6)])
        odd = linear([(math.sin(2 * math.pi * k * a / 16), o[a]) for a in (1, 3, 5, 7)])
        if even is None:
            out[k] = odd
        else:
            out[k] = odd + even
            out[8 - k] = odd - even
    return out


def fft(values, sign):
    count = len(values)
    if count == 1:
        return values
    if count == 2:
        (ar, ai), (br, bi) = values
        return [(ar + br, ai + bi), (ar - br, ai - bi)]
    if count == 4:
        (ar, ai), (br, bi), (cr, ci), (dr, di) = values
        sr, si, tr, ti = ar + cr, ai + ci, ar - cr, ai - ci
        ur, ui, vr, vi = br + dr, bi + di, br - dr, bi - di
        if sign > 0:
            return [(sr + ur, si + ui), (tr - vi, ti + vr), (sr - ur, si - ui), (tr + vi, ti - vr)]
        return [(sr + ur, si + ui), (tr + vi, ti - vr), (sr - ur, si - ui), (tr - vi, ti + vr)]
    quarter = count // 4
    parts = [fft(values[n::4], sign) for n in range(4)]
    out = [None] * count
    for k in range(quarter):
        four = []
        for n in range(4):
            re, im = parts[n][k]
            angle = sign * 2 * math.pi * n * k / count
            c, s = math.cos(angle), math.sin(angle)
            if n * k == 0:
                four.append((re, im))
            elif abs(abs(c) - abs(s)) < 1e-9:
                h = abs(c)
                cs, ss = math.copysign(1, c), math.copysign(1, s)
                r = (re if cs > 0 else -re) - (im if ss > 0 else -im)
                i = (im if cs > 0 else -im) + (re if ss > 0 else -re)
                four.append((h * r, h * i))
            else:
                four.append((re * c - im * s, re * s + im * c))
        for m, value in enumerate(fft(four, sign)):
            out[k + m * quarter] = value
    return out


def split(value):
    high = value.astype(BF16)
    return high, (value - high.astype(F32)).astype(BF16)


def dot3(a, b, dims):
    (ah, al), (bh, bl) = a, b
    dot = functools.partial(
        lax.dot_general, dimension_numbers=(dims, ((), ())), preferred_element_type=F32
    )
    return dot(ah, bh) + (dot(al, bh) + dot(ah, bl))


def tables():
    m = np.arange(128)
    rows = np.zeros((256, 256))
    for d in range(32):
        for jj in range(4):
            angle = 2 * np.pi * ((4 * d + jj) * m % 128) / 128
            rows[8 * d + jj] = np.concatenate([np.cos(angle), np.sin(angle)])
            rows[8 * d + 4 + jj] = np.concatenate([-np.sin(angle), np.cos(angle)])
    n = np.arange(64)
    angle = 2 * np.pi * (n[:, None] * n[None, :] % 64) / 64
    cols = np.zeros((2, 2, 64, 2, 2, 64))
    for kk in range(2):
        cols[0, kk, :, 0, kk] = np.cos(angle)
        cols[1, kk, :, 0, kk] = np.sin(angle)
        cols[0, kk, :, 1, kk] = -np.sin(angle)
        cols[1, kk, :, 1, kk] = np.cos(angle)
    cols = cols.reshape(256, 256)
    early = np.concatenate([np.arange(16), np.arange(48, 64)])
    chunk = np.concatenate([early, np.arange(16, 48)]).reshape(2, 32)
    back = cols.T.reshape(256, 2, 2, 64)[:, :, :, chunk]
    back = back.transpose(0, 1, 3, 2, 4).reshape(256, 256)
    k = np.arange(1, 9)
    angle = -2 * np.pi * k[:, None] * m[None, :] / 2048
    row_twist = np.concatenate([np.cos(angle), np.sin(angle)])
    u1 = np.arange(32)
    angle = -2 * np.pi * u1[:, None] * n[None, :] / 2048
    angle = np.concatenate([angle, angle], axis=1)
    lanes = np.broadcast_to(chunk[:, None, :], (2, 2, 32)).reshape(128)
    turned = -2 * np.pi * u1[:, None] * lanes[None, :] / 2048
    col_twist = np.stack([np.cos(angle), np.sin(angle), np.cos(turned), np.sin(turned)])

    flip = np.zeros((2, 2, 128, 128))
    for kk in range(2):
        for u in range(64):
            flip[0, :, 64 * kk + 63 - u, 64 * kk + u] = 1.0
            flip[1, :, 64 * kk + (64 - u) % 64, 64 * kk + u] = 1.0
    pick = np.zeros((2, 40, 2, 64))
    for kk in range(2):
        for q in range(3):
            for half in range(2):
                s = 4 * q + 2 * half + kk
                k = s + 1 if s < 8 else 0
                for jj in range(4):
                    if s < 9:
                        pick[kk, 8 * q + 4 * half + jj, :, 16 * jj + k] = 2.0**-22
                    if s < 7:
                        pick[kk, 24 + 8 * q + 4 * half + jj, :, 16 * (3 - jj) + 16 - k] = 2.0**-22
    perm = np.concatenate([flip.reshape(512, 128), pick.reshape(80, 128)]).astype(BF16)

    def halves(table):
        high = table.astype(BF16)
        return np.stack([high, (table - high.astype(np.float64)).astype(BF16)])

    return (
        halves(rows),
        halves(cols),
        halves(back),
        np.asarray(row_twist, np.float32),
        np.asarray(col_twist, np.float32),
        perm,
    )


def roll(value, shift, axis):
    return pltpu.roll(value, shift % value.shape[axis], axis)


hops = ((2, 2), (1, 1), (3, 3), (1, 3), (3, 1), (2, 1), (1, 2), (2, 3))
hops = hops + ((3, 2), (2, 0), (0, 2), (1, 0), (0, 1), (3, 0), (0, 3), (0, 0))


def others(p):
    core, x, y = lax.rem(p, 2), lax.rem(p // 2, 4), p // 8
    for far in (0, 1):
        for dy, dx in hops:
            if (dy, dx, far) != (0, 0, 0):
                yield lax.rem(y + dy, 4) * 8 + lax.rem(x + dx, 4) * 2 + lax.rem(core + far, 2)


def drain(ref, sem):
    pltpu.make_async_copy(ref, ref, sem).wait()


def kernel(
    est_in, dirty_in, psf_in, row_table_in, col_table_in, col_back_in, row_twist_in, col_twist_in,
    perm_in,
    shrink_ref, blur_ref,
    est, dirty, psf_wide, row_table, col_table, col_back, row_twist, col_twist, perm,
    psf, abuf, send, recv, spec, send_a, send_b, recv_a, recv_b,
    hz, hh, hp, hpr, hr, smooth_a, smooth_b, det, energy, ob, mx_own, mx_z, mx_r, blur,
    weights, mirror, flipped, mirror_in, in_sems, sems,
):
    z = lax.axis_index("chan")
    p = lax.axis_index("rows")

    barrier = pltpu.get_barrier_semaphore()

    def greet_row(i, carry):
        pl.semaphore_signal(
            barrier, inc=1, device_id={"rows": lax.rem(p + i, R)}, device_id_type=MESH
        )
        return carry

    def greet_chan(i, carry):
        pl.semaphore_signal(
            barrier, inc=1, device_id={"chan": lax.rem(z + i, Z)}, device_id_type=MESH
        )
        return carry

    lax.fori_loop(1, R, greet_row, 0)
    lax.fori_loop(1, Z, greet_chan, 0)

    pairs = (
        (est_in, est), (row_twist_in, row_twist), (row_table_in, row_table), (psf_in, psf_wide),
        (perm_in, perm), (col_twist_in, col_twist), (col_table_in, col_table),
        (col_back_in, col_back), (dirty_in, dirty),
    )
    loads = [pltpu.make_async_copy(a, b, in_sems.at[i]) for i, (a, b) in enumerate(pairs)]
    for load in loads:
        load.start()

    def remote(source, target, send_sem, recv_sem, **device):
        return pltpu.make_async_remote_copy(
            src_ref=source,
            dst_ref=target,
            send_sem=sems.at[send_sem],
            recv_sem=sems.at[recv_sem],
            device_id=device,
            device_id_type=MESH,
        )

    abuf[576:640, :] = jnp.zeros((64, 256), F32)
    for load in loads[:3]:
        load.wait()

    def rows_forward(g, carry):
        at = pl.ds(pl.multiple_of(8 * g, 8), 8)
        x = [est[at, 128 * a : 128 * a + 128] for a in range(16)]
        e = [None] + [x[a] + x[16 - a] for a in range(1, 8)]
        o = [None] + [x[a] - x[16 - a] for a in range(1, 8)]
        re = cosine_16(x[0], x[8], e)
        im = sine_16(o)
        for k in range(1, 9):
            c = row_twist[k - 1 : k, :]
            s = row_twist[k + 7 : k + 8, :]
            to = pl.ds(pl.multiple_of(64 * (k - 1) + 8 * g, 8), 8)
            if k < 8:
                abuf[to, 0:128] = re[k] * c + im[k] * s
                abuf[to, 128:256] = re[k] * s - im[k] * c
            else:
                abuf[to, 0:128] = re[k] * c
                abuf[to, 128:256] = re[k] * s
        to = pl.ds(pl.multiple_of(512 + 8 * g, 8), 8)
        abuf[to, 0:128] = re[0]
        abuf[to, 128:256] = jnp.zeros((8, 128), F32)
        return carry

    lax.fori_loop(0, 8, rows_forward, 0)
    table = (row_table[0], row_table[1])
    for t in range(TILES):
        out = dot3(table, split(abuf[128 * t : 128 * t + 128, :]), ((1,), (1,)))
        send[:, t] = out.reshape(R, 8, 128)

    left_half = lax.broadcasted_iota(jnp.int32, (40, 128), 1) < 64
    for load in loads[3:5]:
        load.wait()
    for b in range(16):
        psf[128 * b : 128 * b + 128, :] = jnp.transpose(psf_wide[:, 128 * b : 128 * b + 128])
    for i in range(8):
        rows = [psf[pl.ds(4 * i + n, 64, stride=32), :] for n in range(4)]
        high, low = split(jnp.concatenate(rows, axis=0))
        both = jnp.concatenate([high, low], axis=1)
        out = lax.dot_general(
            perm[512:592], both, (((1,), (1,)), ((), ())), preferred_element_type=F32
        )
        for n in range(2):
            a = out[0:40, 128 * n : 128 * n + 128]
            b = out[40:80, 128 * n : 128 * n + 128]
            first = jnp.where(left_half, a, roll(b, 64, 1))
            second = jnp.where(left_half, roll(a, 64, 1), b)
            for u1, value in ((4 * i + 2 * n, first), (4 * i + 2 * n + 1, second)):
                for q in range(3):
                    weights[q, u1] = value[8 * q : 8 * q + 8]
                for q in range(2):
                    mirror[q, u1] = value[24 + 8 * q : 32 + 8 * q]
    for q in range(2):
        high, low = split(mirror[q].reshape(256, 128))
        both = jnp.concatenate([high, low], axis=1)
        out = jnp.dot(both, perm[0:256], preferred_element_type=F32)
        zero = jnp.dot(both[0:16], perm[256:512], preferred_element_type=F32)
        flipped[q, 0] = zero[0:8]
        for u1 in range(1, 32):
            flipped[q, 32 - u1] = out[8 * u1 : 8 * u1 + 8]

    pl.semaphore_wait(barrier, R - 1 + Z - 1)

    for to in others(p):
        remote(send.at[to], recv.at[p, 0:TILES], 2, 3, rows=to).start()

    def partner(q):
        return remote(flipped.at[q], mirror_in.at[q], 26 + q, q, rows=R - 1 - p)

    partner(0).start()
    partner(1).start()
    recv[p, 0:TILES] = send[p]
    recv[:, TILES] = jnp.zeros((R, 8, 128), F32)
    for load in loads[5:]:
        load.wait()
    drain(recv.at[0 : R - 1, 0:TILES], sems.at[3])
    drain(send.at[0 : R - 1], sems.at[2])

    upper = lax.broadcasted_iota(jnp.int32, (8, 128), 0) < 4
    left = lax.broadcasted_iota(jnp.int32, (8, 128), 1) < 64

    def columns_forward(q):
        values = []
        for i in range(R):
            a = recv[i, 2 * q]
            b = recv[i, 2 * q + 1]
            values.append(
                (jnp.where(upper, a, roll(b, 4, 0)), jnp.where(upper, roll(a, 4, 0), b))
            )
        for u, (re, im) in enumerate(fft(values, -1)):
            c = col_twist[0, u : u + 1, :]
            s = col_twist[1, u : u + 1, :]
            spec[q, 8 * u : 8 * u + 8, 0:128] = re * c - im * s
            spec[q, 8 * u : 8 * u + 8, 128:256] = re * s + im * c
        spec[q] = dot3(split(spec[q]), (col_table[0], col_table[1]), ((1,), (0,)))

    def columns_inverse(q, w):
        out = spec[q]
        w = w.reshape(256, 128)
        out = jnp.concatenate([out[:, 0:128] * w, out[:, 128:256] * w], axis=1)
        spec[q] = dot3(split(out), (col_back[0], col_back[1]), ((1,), (0,)))
        values = []
        for u in range(R):
            c = col_twist[2, u : u + 1, :]
            s = col_twist[3, u : u + 1, :]
            re = spec[q, 8 * u : 8 * u + 8, 0:128]
            im = spec[q, 8 * u : 8 * u + 8, 128:256]
            values.append((re * c + im * s, im * c - re * s))
        whole = jnp.logical_or(left, q == 2)
        for i, (re, im) in enumerate(fft(values, 1)):
            a = jnp.where(upper, re, roll(im, 4, 0))
            b = jnp.where(upper, roll(re, 4, 0), im)
            send_a[i, q] = jnp.where(whole, a, roll(b, 64, 1))
            send_b[i, q] = jnp.where(left, roll(a, 64, 1), b)

        for to in others(p):
            remote(send_a.at[to, q], recv_a.at[p, q], 4, 5, rows=to).start()

    def one_forward(q, carry):
        columns_forward(q)
        return carry

    def one_inverse(q, carry):
        partner(q).wait_recv()
        columns_inverse(q, weights[q] + mirror_in[q])
        return carry

    columns_forward(2)
    columns_inverse(2, weights[2])
    lax.fori_loop(0, 2, one_forward, 0)
    lax.fori_loop(0, 2, one_inverse, 0)
    partner(0).wait_send()
    partner(1).wait_send()
    for to in others(p):
        remote(send_b.at[to, 0:2], recv_b.at[p], 6, 7, rows=to).start()
    recv_a[p] = send_a[p]
    recv_b[p] = send_b[p, 0:2]

    def rows_inverse(base, spread, first, last):
        def group(g, carry):
            re, im = [None] * 9, [None] * 8
            for k in range(1, 9):
                c = row_twist[k - 1 : k, :]
                s = row_twist[k + 7 : k + 8, :]
                to = pl.ds(pl.multiple_of(base + 32 * (k - 1) + 8 * g, 8), 8)
                gr, gi = abuf[to, 0:128], abuf[to, 128:256]
                re[k] = gr * c + gi * s
                if k < 8:
                    im[k] = gi * c - gr * s
            re[0] = abuf[pl.ds(pl.multiple_of(last + 8 * g, 8), 8), 0:128]
            cosine = cosine_16(re[0], re[8], re)
            sine = sine_16(im)
            at = pl.ds(pl.multiple_of(first + 8 * g + spread * (g // 2), 8), 8)
            edges = {}
            for a in range(16):
                if a == 0 or a == 8:
                    blurred = cosine[a]
                elif a < 8:
                    blurred = cosine[a] - sine[a]
                else:
                    blurred = cosine[16 - a] + sine[16 - a]
                lanes = slice(128 * a, 128 * a + 128)
                blur[at, lanes] = blurred
                halfway = est[at, lanes] + step_size * (dirty[at, lanes] - blurred)
                hz[a // 4, a % 4, at, :] = halfway
                if a % 4 in (0, 3):
                    edges[a] = halfway
            none = jnp.zeros((8, 128), F32)
            for c in range(Z):
                after = edges[4 * c + 4] if c < Z - 1 else none
                before = edges[4 * c - 1] if c > 0 else none
                hh[c, at, :] = roll(jnp.where(left, after, before), 16, 1)
            return carry

        lax.fori_loop(0, 4, group, 0)

    lane_16 = lax.broadcasted_iota(jnp.int32, (16, 128), 1)

    def pack(half, groups):
        for c in range(Z):
            a, b = (hh[c, 16 * g : 16 * g + 16, :] for g in groups)
            hp[half, c] = jnp.where(lane_16 < 32, a, roll(b, 32, 1))

    def unpack(half, groups):
        for c in range(Z):
            for e, g in enumerate(groups):
                hr[c, 4, 24 + 16 * g : 40 + 16 * g, :] = roll(hpr[half, c], -32 * e - 16, 1)

    drain(recv_a.at[0 : R - 1], sems.at[5])
    for t in range(3):
        block = recv_a[:, t].reshape(256, 128)
        abuf[128 * t : 128 * t + 128, :] = dot3(split(block), table, ((0,), (0,)))
    rows_inverse(0, 32, 0, 256)
    pack(0, (0, 3))
    for i in (2, 1, 3):
        to = lax.rem(z + i, Z)
        for r in (0, 48):
            remote(
                hz.at[to, :, r : r + 16], hr.at[z, 0:4, r + 24 : r + 40], 8, 9, chan=to
            ).start()
        remote(hp.at[0, to], hpr.at[0, z], 10, 11, chan=to).start()

    drain(recv_b.at[0 : R - 1], sems.at[7])
    for t in range(2):
        block = recv_b[:, t].reshape(256, 128)
        abuf[384 + 128 * t : 512 + 128 * t, :] = dot3(split(block), table, ((0,), (0,)))
    rows_inverse(384, 0, 16, 320)
    pack(1, (1, 2))
    blur_out = pltpu.make_async_copy(blur, blur_ref, sems.at[29])
    blur_out.start()
    for i in (2, 1, 3):
        to = lax.rem(z + i, Z)
        remote(hz.at[to, :, 16:48], hr.at[z, 0:4, 40:72], 12, 13, chan=to).start()
        remote(hp.at[1, to], hpr.at[1, z], 14, 15, chan=to).start()
    drain(send_a.at[0 : R - 1], sems.at[4])
    drain(send_b.at[0 : R - 1, 0:2], sems.at[6])
    hr[z, 0:4, 24:88] = hz[z]
    hpr[:, z] = hp[:, z]

    hr[:, :, 0:8, :] = jnp.zeros((Z, 5, 8, 128), F32)
    hr[:, :, 104:112, :] = jnp.zeros((Z, 5, 8, 128), F32)

    @pl.when(p == 0)
    def _():
        hr[:, :, 8:24, :] = jnp.zeros((Z, 5, 16, 128), F32)

    @pl.when(p == R - 1)
    def _():
        hr[:, :, 88:104, :] = jnp.zeros((Z, 5, 16, 128), F32)

    drain(hz.at[0 : Z - 1, :, 0:32], sems.at[9])
    drain(hp.at[0, 0 : Z - 1], sems.at[11])
    unpack(0, (0, 3))
    above = remote(hr.at[:, :, 24:40], hr.at[:, :, 88:104], 16, 17, rows=lax.rem(p + R - 1, R))
    below = remote(hr.at[:, :, 72:88], hr.at[:, :, 8:24], 18, 19, rows=lax.rem(p + 1, R))

    @pl.when(p > 0)
    def _():
        above.start()

    @pl.when(p < R - 1)
    def _():
        below.start()

    drain(hz.at[0 : Z - 1, :, 0:32], sems.at[13])
    drain(hp.at[0, 0 : Z - 1], sems.at[15])
    unpack(1, (1, 2))
    drain(hz.at[0 : Z - 1, :, 0:32], sems.at[8])
    drain(hp.at[0, 0 : Z - 1], sems.at[10])
    drain(hz.at[0 : Z - 1, :, 0:32], sems.at[12])
    drain(hp.at[0, 0 : Z - 1], sems.at[14])

    @pl.when(p < R - 1)
    def _():
        above.wait_recv()

    @pl.when(p > 0)
    def _():
        below.wait_recv()
        above.wait_send()

    @pl.when(p < R - 1)
    def _():
        below.wait_send()


    lane_8 = lax.broadcasted_iota(jnp.int32, (8, 128), 1)
    top = jnp.where(p > 0, 1.0, 0.0)
    bottom = jnp.where(p < R - 1, 1.0, 0.0)
    side = jnp.where(
        lane_8 < 64, jnp.where(z < Z - 1, 1.0, 0.0), jnp.where(z > 0, 1.0, 0.0)
    )

    def down(source, t, row, spacing):
        x = [source[t, row + k * spacing : row + k * spacing + 8, :] for k in range(-2, 3)]
        near, far = x[1] + x[3], x[0] + x[4]
        return far * (1 / 256) + (x[2] * (6 / 256) + near * (4 / 256))

    def along(x, spacing):
        for step in range(4):
            if step % 2 == 0:
                turned = [roll(v, spacing, 1) for v in x]
                x = [
                    x[t] + jnp.where(lane_8 < spacing, turned[t - 1], turned[t]) for t in range(5)
                ]
            else:
                turned = [roll(v, -spacing, 1) for v in x]
                x = [
                    x[t] + jnp.where(lane_8 >= 128 - spacing, turned[(t + 1) % 5], turned[t])
                    for t in range(5)
                ]
        return x

    def starlet(ch, carry):
        for level, (start, stop) in enumerate(((0, 12), (1, 11), (2, 10))):
            source = (hr.at[ch], smooth_a, smooth_b)[level]
            target = (smooth_a, smooth_b, None)[level]
            for i in range(start, stop):
                rows = slice(8 * i + 8, 8 * i + 16)
                x = along([down(source, t, 8 * i + 8, 1 << level) for t in range(5)], 1 << level)
                if target is not None:
                    if i < 2:
                        x = [v * top for v in x]
                    if i >= 10:
                        x = [v * bottom for v in x]
                    x[4] = x[4] * side
                    for t in range(5):
                        target[t, rows, :] = x[t]
                if 2 <= i < 10:
                    at = slice(8 * i - 16, 8 * i - 8)
                    for t in range(4):
                        detail = source[t, rows, :] - x[t]
                        det[level, ch, t, at, :] = detail
                        energy[level, t, at, :] = energy[level, t, at, :] + detail * detail
        return carry

    energy[...] = jnp.zeros((3, 4, 64, 128), F32)
    lax.fori_loop(0, Z, starlet, 0)

    peaks = jnp.concatenate(
        [
            jnp.max(jnp.max(energy[level], axis=0), axis=0, keepdims=True)
            for level in range(3)
        ],
        axis=1,
    )
    mx_own[0] = peaks
    for i in range(1, Z):
        remote(mx_own.at[0], mx_z.at[z], 20, 21, chan=lax.rem(z + i, Z)).start()
    mx_z[z] = peaks
    drain(mx_z.at[0 : Z - 1], sems.at[21])
    peaks = jnp.max(mx_z[...], axis=0)
    mx_own[1] = peaks

    def begin_max(i, carry):
        remote(mx_own.at[1], mx_r.at[p], 22, 23, rows=lax.rem(p + i, R)).start()
        return carry

    lax.fori_loop(1, R, begin_max, 0)
    mx_r[p] = peaks
    energy[...] = lax.rsqrt(energy[...])
    drain(mx_r.at[0 : R - 1], sems.at[23])
    drain(mx_r.at[0 : R - 1], sems.at[22])
    drain(mx_z.at[0 : Z - 1], sems.at[20])
    peaks = jnp.sqrt(jnp.max(mx_r[...], axis=0))
    for level in range(3):
        peak = jnp.max(peaks[:, 128 * level : 128 * level + 128], axis=1, keepdims=True)
        energy[level] = jnp.minimum(energy[level] * (fractions[level] * peak), 1.0)

    def shrunk(ch):
        for t in range(4):
            out = energy[0, t] * det[0, ch, t]
            out = out + energy[1, t] * det[1, ch, t]
            ob[ch, :, 128 * t : 128 * t + 128] = out + energy[2, t] * det[2, ch, t]

    block = pl.ds(pl.multiple_of(512 * z, 512), 512)

    def final(i, carry):
        ch = lax.rem(z + 2 - (i // 2) + 2 * (i // 3), Z)
        shrunk(ch)
        remote(ob.at[ch], shrink_ref.at[:, block], 24, 25, chan=ch).start()
        return carry

    lax.fori_loop(1, Z, final, 0)
    shrunk(z)
    own = pltpu.make_async_copy(ob.at[z], shrink_ref.at[:, block], sems.at[28])
    own.start()
    drain(ob.at[0 : Z - 1], sems.at[25])
    drain(ob.at[0 : Z - 1], sems.at[24])
    own.wait()
    blur_out.wait()


def shards(estimate, dirty_image, psf_weights):
    constants = tables()
    arguments = (estimate[0], dirty_image[0], psf_weights[0].T, *constants)
    anywhere = pl.BlockSpec(memory_space=pl.ANY)
    block = jax.ShapeDtypeStruct((64, 2048), F32)
    dma = pltpu.SemaphoreType.DMA
    shapes = [
        (2048, 64),
        (640, 256),
        (R, TILES, 8, 128),
        (R, TILES + 1, 8, 128),
        (3, 256, 256),
        (R, 3, 8, 128),
        (R, 3, 8, 128),
        (R, 3, 8, 128),
        (R, 2, 8, 128),
        (Z, 4, 64, 128),
        (Z, 64, 128),
        (2, Z, 16, 128),
        (2, Z, 16, 128),
        (Z, 5, 112, 128),
        (5, 112, 128),
        (5, 112, 128),
        (3, Z, 4, 64, 128),
        (3, 4, 64, 128),
        (Z, 64, 512),
        (2, 1, 384),
        (Z, 1, 384),
        (R, 1, 384),
        (64, 2048),
        (3, 32, 8, 128),
        (2, 32, 8, 128),
        (2, 32, 8, 128),
        (2, 32, 8, 128),
    ]
    shrink, blurred = pl.pallas_call(
        kernel,
        out_shape=(block, block),
        in_specs=[anywhere] * len(arguments),
        out_specs=(anywhere, anywhere),
        scratch_shapes=[pltpu.VMEM(a.shape, a.dtype) for a in arguments]
        + [pltpu.VMEM(shape, F32) for shape in shapes]
        + [dma((len(arguments),)), dma((30,))],
        compiler_params=pltpu.CompilerParams(
            collective_id=0, has_side_effects=True, vmem_limit_bytes=VMEM_LIMIT
        ),
    )(*arguments)
    residual = dirty_image[0] - blurred
    new = estimate[0] + step_size * residual - shrink
    return (new[None], residual[None])


def solution(mesh):
    return jax.shard_map(
        shards,
        mesh=mesh,
        in_specs=(P("chan", "rows", None), P("chan", "rows", None), P("chan", None, "rows")),
        out_specs=(P("chan", "rows", None), P("chan", "rows", None)),
        check_vma=False,
    )
```

```python
import functools
import math

import jax
import jax.numpy as jnp
import numpy as np
from jax import lax
from jax.experimental import pallas as pl
from jax.experimental.pallas import tpu as pltpu
from jax.sharding import PartitionSpec as P

fractions = (0.03, 0.02, 0.015)
step_size = 0.9
MESH = pl.DeviceIdType.MESH
F32 = jnp.float32
BF16 = jnp.bfloat16
R = 32
Z = 4
VMEM_LIMIT = 60 * 1024 * 1024
TILES = 5


def linear(pairs):
    total = None
    for coef, value in pairs:
        if abs(coef) < 1e-12:
            continue
        if abs(coef - 1.0) < 1e-12:
            total = value if total is None else total + value
        elif abs(coef + 1.0) < 1e-12:
            total = -value if total is None else total - value
        else:
            term = coef * value
            total = term if total is None else total + term
    return total


def cosine_16(first, middle, e):
    out = [None] * 9
    for k in range(5):
        even = linear(
            [(1.0, first), (1.0 if k % 2 == 0 else -1.0, middle)]
            + [(math.cos(2 * math.pi * k * a / 16), e[a]) for a in (2, 4, 6)]
        )
        odd = linear([(math.cos(2 * math.pi * k * a / 16), e[a]) for a in (1, 3, 5, 7)])
        if odd is None:
            out[k] = even
            out[8 - k] = even
        else:
            out[k] = even + odd
            out[8 - k] = even - odd
    return out


def sine_16(o):
    out = [None] * 8
    for k in range(1, 5):
        even = linear([(math.sin(2 * math.pi * k * a / 16), o[a]) for a in (2, 4, 6)])
        odd = linear([(math.sin(2 * math.pi * k * a / 16), o[a]) for a in (1, 3, 5, 7)])
        if even is None:
            out[k] = odd
        else:
            out[k] = odd + even
            out[8 - k] = odd - even
    return out


def fft(values, sign):
    count = len(values)
    if count == 1:
        return values
    if count == 2:
        (ar, ai), (br, bi) = values
        return [(ar + br, ai + bi), (ar - br, ai - bi)]
    if count == 4:
        (ar, ai), (br, bi), (cr, ci), (dr, di) = values
        sr, si, tr, ti = ar + cr, ai + ci, ar - cr, ai - ci
        ur, ui, vr, vi = br + dr, bi + di, br - dr, bi - di
        if sign > 0:
            return [(sr + ur, si + ui), (tr - vi, ti + vr), (sr - ur, si - ui), (tr + vi, ti - vr)]
        return [(sr + ur, si + ui), (tr + vi, ti - vr), (sr - ur, si - ui), (tr - vi, ti + vr)]
    quarter = count // 4
    parts = [fft(values[n::4], sign) for n in range(4)]
    out = [None] * count
    for k in range(quarter):
        four = []
        for n in range(4):
            re, im = parts[n][k]
            angle = sign * 2 * math.pi * n * k / count
            c, s = math.cos(angle), math.sin(angle)
            if n * k == 0:
                four.append((re, im))
            elif abs(abs(c) - abs(s)) < 1e-9:
                h = abs(c)
                cs, ss = math.copysign(1, c), math.copysign(1, s)
                r = (re if cs > 0 else -re) - (im if ss > 0 else -im)
                i = (im if cs > 0 else -im) + (re if ss > 0 else -re)
                four.append((h * r, h * i))
            else:
                four.append((re * c - im * s, re * s + im * c))
        for m, value in enumerate(fft(four, sign)):
            out[k + m * quarter] = value
    return out


def split(value):
    high = value.astype(BF16)
    return high, (value - high.astype(F32)).astype(BF16)


def dot3(a, b, dims):
    (ah, al), (bh, bl) = a, b
    dot = functools.partial(
        lax.dot_general, dimension_numbers=(dims, ((), ())), preferred_element_type=F32
    )
    return dot(ah, bh) + (dot(al, bh) + dot(ah, bl))


def tables():
    m = np.arange(128)
    rows = np.zeros((256, 256))
    for d in range(32):
        for jj in range(4):
            angle = 2 * np.pi * ((4 * d + jj) * m % 128) / 128
            rows[8 * d + jj] = np.concatenate([np.cos(angle), np.sin(angle)])
            rows[8 * d + 4 + jj] = np.concatenate([-np.sin(angle), np.cos(angle)])
    n = np.arange(64)
    angle = 2 * np.pi * (n[:, None] * n[None, :] % 64) / 64
    cols = np.zeros((2, 2, 64, 2, 2, 64))
    for kk in range(2):
        cols[0, kk, :, 0, kk] = np.cos(angle)
        cols[1, kk, :, 0, kk] = np.sin(angle)
        cols[0, kk, :, 1, kk] = -np.sin(angle)
        cols[1, kk, :, 1, kk] = np.cos(angle)
    cols = cols.reshape(256, 256)
    early = np.concatenate([np.arange(16), np.arange(48, 64)])
    chunk = np.concatenate([early, np.arange(16, 48)]).reshape(2, 32)
    back = cols.T.reshape(256, 2, 2, 64)[:, :, :, chunk]
    back = back.transpose(0, 1, 3, 2, 4).reshape(256, 256)
    k = np.arange(1, 9)
    angle = -2 * np.pi * k[:, None] * m[None, :] / 2048
    row_twist = np.concatenate([np.cos(angle), np.sin(angle)])
    u1 = np.arange(32)
    angle = -2 * np.pi * u1[:, None] * n[None, :] / 2048
    angle = np.concatenate([angle, angle], axis=1)
    lanes = np.broadcast_to(chunk[:, None, :], (2, 2, 32)).reshape(128)
    turned = -2 * np.pi * u1[:, None] * lanes[None, :] / 2048
    col_twist = np.stack([np.cos(angle), np.sin(angle), np.cos(turned), np.sin(turned)])

    flip = np.zeros((2, 2, 128, 128))
    for kk in range(2):
        for u in range(64):
            flip[0, :, 64 * kk + 63 - u, 64 * kk + u] = 1.0
            flip[1, :, 64 * kk + (64 - u) % 64, 64 * kk + u] = 1.0
    pick = np.zeros((2, 40, 2, 64))
    for kk in range(2):
        for q in range(3):
            for half in range(2):
                s = 4 * q + 2 * half + kk
                k = s + 1 if s < 8 else 0
                for jj in range(4):
                    if s < 9:
                        pick[kk, 8 * q + 4 * half + jj, :, 16 * jj + k] = 2.0**-22
                    if s < 7:
                        pick[kk, 24 + 8 * q + 4 * half + jj, :, 16 * (3 - jj) + 16 - k] = 2.0**-22
    perm = np.concatenate([flip.reshape(512, 128), pick.reshape(80, 128)]).astype(BF16)

    def halves(table):
        high = table.astype(BF16)
        return np.stack([high, (table - high.astype(np.float64)).astype(BF16)])

    return (
        halves(rows),
        halves(cols),
        halves(back),
        np.asarray(row_twist, np.float32),
        np.asarray(col_twist, np.float32),
        perm,
    )


def roll(value, shift, axis):
    return pltpu.roll(value, shift % value.shape[axis], axis)


hops = ((2, 2), (1, 1), (3, 3), (1, 3), (3, 1), (2, 1), (1, 2), (2, 3))
hops = hops + ((3, 2), (2, 0), (0, 2), (1, 0), (0, 1), (3, 0), (0, 3), (0, 0))


def others(p):
    core, x, y = lax.rem(p, 2), lax.rem(p // 2, 4), p // 8
    for far in (0, 1):
        for dy, dx in hops:
            if (dy, dx, far) != (0, 0, 0):
                yield lax.rem(y + dy, 4) * 8 + lax.rem(x + dx, 4) * 2 + lax.rem(core + far, 2)


def drain(ref, sem):
    pltpu.make_async_copy(ref, ref, sem).wait()


def kernel(
    est_in, dirty_in, psf_in, row_table_in, col_table_in, col_back_in, row_twist_in, col_twist_in,
    perm_in,
    shrink_ref, blur_ref,
    est, dirty, psf_wide, row_table, col_table, col_back, row_twist, col_twist, perm,
    psf, abuf, send, recv, spec, send_a, send_b, recv_a, recv_b,
    hz, hh, hp, hpr, hr, rows_done, smooth_a, smooth_b, det, energy, ob, mx_own, mx_z, mx_r, blur,
    weights, mirror, flipped, mirror_in, in_sems, sems,
):
    z = lax.axis_index("chan")
    p = lax.axis_index("rows")

    barrier = pltpu.get_barrier_semaphore()

    def greet_row(i, carry):
        pl.semaphore_signal(
            barrier, inc=1, device_id={"rows": lax.rem(p + i, R)}, device_id_type=MESH
        )
        return carry

    def greet_chan(i, carry):
        pl.semaphore_signal(
            barrier, inc=1, device_id={"chan": lax.rem(z + i, Z)}, device_id_type=MESH
        )
        return carry

    lax.fori_loop(1, R, greet_row, 0)
    lax.fori_loop(1, Z, greet_chan, 0)

    pairs = (
        (est_in, est), (row_twist_in, row_twist), (row_table_in, row_table), (psf_in, psf_wide),
        (perm_in, perm), (col_twist_in, col_twist), (col_table_in, col_table),
        (col_back_in, col_back), (dirty_in, dirty),
    )
    loads = [pltpu.make_async_copy(a, b, in_sems.at[i]) for i, (a, b) in enumerate(pairs)]
    for load in loads:
        load.start()

    def remote(source, target, send_sem, recv_sem, **device):
        return pltpu.make_async_remote_copy(
            src_ref=source,
            dst_ref=target,
            send_sem=sems.at[send_sem],
            recv_sem=sems.at[recv_sem],
            device_id=device,
            device_id_type=MESH,
        )

    abuf[576:640, :] = jnp.zeros((64, 256), F32)
    for load in loads[:3]:
        load.wait()

    def rows_forward(g, carry):
        at = pl.ds(pl.multiple_of(8 * g, 8), 8)
        x = [est[at, 128 * a : 128 * a + 128] for a in range(16)]
        e = [None] + [x[a] + x[16 - a] for a in range(1, 8)]
        o = [None] + [x[a] - x[16 - a] for a in range(1, 8)]
        re = cosine_16(x[0], x[8], e)
        im = sine_16(o)
        for k in range(1, 9):
            c = row_twist[k - 1 : k, :]
            s = row_twist[k + 7 : k + 8, :]
            to = pl.ds(pl.multiple_of(64 * (k - 1) + 8 * g, 8), 8)
            if k < 8:
                abuf[to, 0:128] = re[k] * c + im[k] * s
                abuf[to, 128:256] = re[k] * s - im[k] * c
            else:
                abuf[to, 0:128] = re[k] * c
                abuf[to, 128:256] = re[k] * s
        to = pl.ds(pl.multiple_of(512 + 8 * g, 8), 8)
        abuf[to, 0:128] = re[0]
        abuf[to, 128:256] = jnp.zeros((8, 128), F32)
        return carry

    lax.fori_loop(0, 8, rows_forward, 0)
    table = (row_table[0], row_table[1])
    for t in range(TILES):
        out = dot3(table, split(abuf[128 * t : 128 * t + 128, :]), ((1,), (1,)))
        send[:, t] = out.reshape(R, 8, 128)

    left_half = lax.broadcasted_iota(jnp.int32, (40, 128), 1) < 64
    for load in loads[3:5]:
        load.wait()
    for b in range(16):
        psf[128 * b : 128 * b + 128, :] = jnp.transpose(psf_wide[:, 128 * b : 128 * b + 128])
    for i in range(8):
        rows = [psf[pl.ds(4 * i + n, 64, stride=32), :] for n in range(4)]
        high, low = split(jnp.concatenate(rows, axis=0))
        both = jnp.concatenate([high, low], axis=1)
        out = lax.dot_general(
            perm[512:592], both, (((1,), (1,)), ((), ())), preferred_element_type=F32
        )
        for n in range(2):
            a = out[0:40, 128 * n : 128 * n + 128]
            b = out[40:80, 128 * n : 128 * n + 128]
            first = jnp.where(left_half, a, roll(b, 64, 1))
            second = jnp.where(left_half, roll(a, 64, 1), b)
            for u1, value in ((4 * i + 2 * n, first), (4 * i + 2 * n + 1, second)):
                for q in range(3):
                    weights[q, u1] = value[8 * q : 8 * q + 8]
                for q in range(2):
                    mirror[q, u1] = value[24 + 8 * q : 32 + 8 * q]
    for q in range(2):
        high, low = split(mirror[q].reshape(256, 128))
        both = jnp.concatenate([high, low], axis=1)
        out = jnp.dot(both, perm[0:256], preferred_element_type=F32)
        zero = jnp.dot(both[0:16], perm[256:512], preferred_element_type=F32)
        flipped[q, 0] = zero[0:8]
        for u1 in range(1, 32):
            flipped[q, 32 - u1] = out[8 * u1 : 8 * u1 + 8]

    pl.semaphore_wait(barrier, R - 1 + Z - 1)

    for to in others(p):
        remote(send.at[to], recv.at[p, 0:TILES], 2, 3, rows=to).start()

    def partner(q):
        return remote(flipped.at[q], mirror_in.at[q], 26 + q, q, rows=R - 1 - p)

    partner(0).start()
    partner(1).start()
    recv[p, 0:TILES] = send[p]
    recv[:, TILES] = jnp.zeros((R, 8, 128), F32)
    for load in loads[5:]:
        load.wait()
    drain(recv.at[0 : R - 1, 0:TILES], sems.at[3])
    drain(send.at[0 : R - 1], sems.at[2])

    upper = lax.broadcasted_iota(jnp.int32, (8, 128), 0) < 4
    left = lax.broadcasted_iota(jnp.int32, (8, 128), 1) < 64

    def columns_forward(q):
        values = []
        for i in range(R):
            a = recv[i, 2 * q]
            b = recv[i, 2 * q + 1]
            values.append(
                (jnp.where(upper, a, roll(b, 4, 0)), jnp.where(upper, roll(a, 4, 0), b))
            )
        for u, (re, im) in enumerate(fft(values, -1)):
            c = col_twist[0, u : u + 1, :]
            s = col_twist[1, u : u + 1, :]
            spec[q, 8 * u : 8 * u + 8, 0:128] = re * c - im * s
            spec[q, 8 * u : 8 * u + 8, 128:256] = re * s + im * c
        spec[q] = dot3(split(spec[q]), (col_table[0], col_table[1]), ((1,), (0,)))

    def columns_inverse(q, w):
        out = spec[q]
        w = w.reshape(256, 128)
        out = jnp.concatenate([out[:, 0:128] * w, out[:, 128:256] * w], axis=1)
        spec[q] = dot3(split(out), (col_back[0], col_back[1]), ((1,), (0,)))
        values = []
        for u in range(R):
            c = col_twist[2, u : u + 1, :]
            s = col_twist[3, u : u + 1, :]
            re = spec[q, 8 * u : 8 * u + 8, 0:128]
            im = spec[q, 8 * u : 8 * u + 8, 128:256]
            values.append((re * c + im * s, im * c - re * s))
        whole = jnp.logical_or(left, q == 2)
        for i, (re, im) in enumerate(fft(values, 1)):
            a = jnp.where(upper, re, roll(im, 4, 0))
            b = jnp.where(upper, roll(re, 4, 0), im)
            send_a[i, q] = jnp.where(whole, a, roll(b, 64, 1))
            send_b[i, q] = jnp.where(left, roll(a, 64, 1), b)

        for to in others(p):
            remote(send_a.at[to, q], recv_a.at[p, q], 4, 5, rows=to).start()

    def one_forward(q, carry):
        columns_forward(q)
        return carry

    def one_inverse(q, carry):
        partner(q).wait_recv()
        columns_inverse(q, weights[q] + mirror_in[q])
        return carry

    columns_forward(2)
    columns_inverse(2, weights[2])
    lax.fori_loop(0, 2, one_forward, 0)
    lax.fori_loop(0, 2, one_inverse, 0)
    partner(0).wait_send()
    partner(1).wait_send()
    for to in others(p):
        remote(send_b.at[to, 0:2], recv_b.at[p], 6, 7, rows=to).start()
    recv_a[p] = send_a[p]
    recv_b[p] = send_b[p, 0:2]

    def rows_inverse(base, spread, first, last):
        def group(g, carry):
            re, im = [None] * 9, [None] * 8
            for k in range(1, 9):
                c = row_twist[k - 1 : k, :]
                s = row_twist[k + 7 : k + 8, :]
                to = pl.ds(pl.multiple_of(base + 32 * (k - 1) + 8 * g, 8), 8)
                gr, gi = abuf[to, 0:128], abuf[to, 128:256]
                re[k] = gr * c + gi * s
                if k < 8:
                    im[k] = gi * c - gr * s
            re[0] = abuf[pl.ds(pl.multiple_of(last + 8 * g, 8), 8), 0:128]
            cosine = cosine_16(re[0], re[8], re)
            sine = sine_16(im)
            at = pl.ds(pl.multiple_of(first + 8 * g + spread * (g // 2), 8), 8)
            edges = {}
            for a in range(16):
                if a == 0 or a == 8:
                    blurred = cosine[a]
                elif a < 8:
                    blurred = cosine[a] - sine[a]
                else:
                    blurred = cosine[16 - a] + sine[16 - a]
                lanes = slice(128 * a, 128 * a + 128)
                blur[at, lanes] = blurred
                halfway = est[at, lanes] + step_size * (dirty[at, lanes] - blurred)
                hz[a // 4, a % 4, at, :] = halfway
                if a % 4 in (0, 3):
                    edges[a] = halfway
            none = jnp.zeros((8, 128), F32)
            for c in range(Z):
                after = edges[4 * c + 4] if c < Z - 1 else none
                before = edges[4 * c - 1] if c > 0 else none
                hh[c, at, :] = roll(jnp.where(left, after, before), 16, 1)
            return carry

        lax.fori_loop(0, 4, group, 0)

    lane_16 = lax.broadcasted_iota(jnp.int32, (16, 128), 1)

    def pack(half, groups):
        for c in range(Z):
            a, b = (hh[c, 16 * g : 16 * g + 16, :] for g in groups)
            hp[half, c] = jnp.where(lane_16 < 32, a, roll(b, 32, 1))

    def unpack(half, groups):
        for c in range(Z):
            for e, g in enumerate(groups):
                hr[c, 4, 24 + 16 * g : 40 + 16 * g, :] = roll(hpr[half, c], -32 * e - 16, 1)

    drain(recv_a.at[0 : R - 1], sems.at[5])
    for t in range(3):
        block = recv_a[:, t].reshape(256, 128)
        abuf[128 * t : 128 * t + 128, :] = dot3(split(block), table, ((0,), (0,)))
    rows_inverse(0, 32, 0, 256)
    pack(0, (0, 3))
    for i in (2, 1, 3):
        to = lax.rem(z + i, Z)
        for r in (0, 48):
            remote(
                hz.at[to, :, r : r + 16], hr.at[z, 0:4, r + 24 : r + 40], 8, 9, chan=to
            ).start()
        remote(hp.at[0, to], hpr.at[0, z], 10, 11, chan=to).start()

    drain(recv_b.at[0 : R - 1], sems.at[7])
    for t in range(2):
        block = recv_b[:, t].reshape(256, 128)
        abuf[384 + 128 * t : 512 + 128 * t, :] = dot3(split(block), table, ((0,), (0,)))
    rows_inverse(384, 0, 16, 320)
    pack(1, (1, 2))
    blur_out = pltpu.make_async_copy(blur, blur_ref, sems.at[29])
    blur_out.start()
    for i in (2, 1, 3):
        to = lax.rem(z + i, Z)
        remote(hz.at[to, :, 16:48], hr.at[z, 0:4, 40:72], 12, 13, chan=to).start()
        remote(hp.at[1, to], hpr.at[1, z], 14, 15, chan=to).start()
    drain(send_a.at[0 : R - 1], sems.at[4])
    drain(send_b.at[0 : R - 1, 0:2], sems.at[6])
    hr[z, 0:4, 24:88] = hz[z]
    hpr[:, z] = hp[:, z]

    hr[:, :, 0:8, :] = jnp.zeros((Z, 5, 8, 128), F32)
    hr[:, :, 104:112, :] = jnp.zeros((Z, 5, 8, 128), F32)

    @pl.when(p == 0)
    def _():
        hr[:, :, 8:24, :] = jnp.zeros((Z, 5, 16, 128), F32)

    @pl.when(p == R - 1)
    def _():
        hr[:, :, 88:104, :] = jnp.zeros((Z, 5, 16, 128), F32)

    drain(hz.at[0 : Z - 1, :, 0:32], sems.at[9])
    drain(hp.at[0, 0 : Z - 1], sems.at[11])
    unpack(0, (0, 3))
    above = remote(hr.at[:, :, 24:40], hr.at[:, :, 88:104], 16, 17, rows=lax.rem(p + R - 1, R))
    below = remote(hr.at[:, :, 72:88], hr.at[:, :, 8:24], 18, 19, rows=lax.rem(p + 1, R))

    @pl.when(p > 0)
    def _():
        above.start()

    @pl.when(p < R - 1)
    def _():
        below.start()

    drain(hz.at[0 : Z - 1, :, 0:32], sems.at[13])
    drain(hp.at[0, 0 : Z - 1], sems.at[15])
    unpack(1, (1, 2))
    drain(hz.at[0 : Z - 1, :, 0:32], sems.at[8])
    drain(hp.at[0, 0 : Z - 1], sems.at[10])
    drain(hz.at[0 : Z - 1, :, 0:32], sems.at[12])
    drain(hp.at[0, 0 : Z - 1], sems.at[14])

    @pl.when(p < R - 1)
    def _():
        above.wait_recv()

    @pl.when(p > 0)
    def _():
        below.wait_recv()
        above.wait_send()

    @pl.when(p < R - 1)
    def _():
        below.wait_send()


    lane_8 = lax.broadcasted_iota(jnp.int32, (8, 128), 1)
    top = jnp.where(p > 0, 1.0, 0.0)
    bottom = jnp.where(p < R - 1, 1.0, 0.0)
    side = jnp.where(
        lane_8 < 64, jnp.where(z < Z - 1, 1.0, 0.0), jnp.where(z > 0, 1.0, 0.0)
    )

    row_8 = lax.broadcasted_iota(jnp.int32, (8, 128), 0)

    def down(x, spacing):
        count = len(x)
        half = [roll(v, 4, 0) for v in x] if spacing > 1 else None
        if spacing > 1:
            half = (
                [half[0]]
                + [jnp.where(row_8 < 4, half[i - 1], half[i]) for i in range(1, count)]
                + [half[-1]]
            )
        if spacing == 4:
            return [None] + [
                (x[i - 1] + x[i + 1]) * (1 / 256)
                + (x[i] * (6 / 256) + (half[i] + half[i + 1]) * (4 / 256))
                for i in range(1, count - 1)
            ]
        if spacing == 2:
            plus = [roll(v, 2, 0) for v in x]
            minus = [roll(v, -2, 0) for v in x]
            out = []
            for i in range(count):
                above = jnp.where(row_8 < 2, plus[max(i - 1, 0)], plus[i])
                below = jnp.where(row_8 >= 6, minus[min(i + 1, count - 1)], minus[i])
                out.append(
                    (half[i] + half[i + 1]) * (1 / 256)
                    + (x[i] * (6 / 256) + (above + below) * (4 / 256))
                )
            return out
        shifted = {}
        for k in (1, -1, 2, -2):
            turned = [roll(v, k, 0) for v in x]
            if k > 0:
                shifted[k] = [
                    jnp.where(row_8 < k, turned[max(i - 1, 0)], turned[i]) for i in range(count)
                ]
            else:
                shifted[k] = [
                    jnp.where(row_8 >= 8 + k, turned[min(i + 1, count - 1)], turned[i])
                    for i in range(count)
                ]
        return [
            (shifted[2][i] + shifted[-2][i]) * (1 / 256)
            + (x[i] * (6 / 256) + (shifted[1][i] + shifted[-1][i]) * (4 / 256))
            for i in range(count)
        ]

    def along(x, spacing):
        total = []
        rolled = {k: [roll(v, k * spacing, 1) for v in x] for k in (1, -1, 2, -2)}
        for t in range(5):
            near = jnp.where(lane_8 < spacing, rolled[1][t - 1], rolled[1][t]) + jnp.where(
                lane_8 >= 128 - spacing, rolled[-1][(t + 1) % 5], rolled[-1][t]
            )
            far = jnp.where(lane_8 < 2 * spacing, rolled[2][t - 1], rolled[2][t]) + jnp.where(
                lane_8 >= 128 - 2 * spacing, rolled[-2][(t + 1) % 5], rolled[-2][t]
            )
            total.append(6.0 * x[t] + (4.0 * near + far))
        return total

    def starlet(ch, carry):
        for level, (start, stop) in enumerate(((0, 12), (1, 11), (2, 10))):
            source = (hr.at[ch], smooth_a, smooth_b)[level]
            target = (smooth_a, smooth_b, None)[level]
            first, last = ((0, 12), (0, 12), (1, 11))[level]
            for t in range(5):
                x = [source[t, 8 * i + 8 : 8 * i + 16, :] for i in range(first, last)]
                x = down(x, 1 << level)
                for i in range(start, stop):
                    rows_done[t, 8 * i + 8 : 8 * i + 16, :] = x[i - first]
            for i in range(start, stop):
                rows = slice(8 * i + 8, 8 * i + 16)
                x = along([rows_done[t, rows, :] for t in range(5)], 1 << level)
                if target is not None:
                    if i < 2:
                        x = [v * top for v in x]
                    if i >= 10:
                        x = [v * bottom for v in x]
                    x[4] = x[4] * side
                    for t in range(5):
                        target[t, rows, :] = x[t]
                if 2 <= i < 10:
                    at = slice(8 * i - 16, 8 * i - 8)
                    for t in range(4):
                        detail = source[t, rows, :] - x[t]
                        det[level, ch, t, at, :] = detail
                        energy[level, t, at, :] = energy[level, t, at, :] + detail * detail
        return carry

    energy[...] = jnp.zeros((3, 4, 64, 128), F32)
    lax.fori_loop(0, Z, starlet, 0)

    peaks = jnp.concatenate(
        [
            jnp.max(jnp.max(energy[level], axis=0), axis=0, keepdims=True)
            for level in range(3)
        ],
        axis=1,
    )
    mx_own[0] = peaks
    for i in range(1, Z):
        remote(mx_own.at[0], mx_z.at[z], 20, 21, chan=lax.rem(z + i, Z)).start()
    mx_z[z] = peaks
    drain(mx_z.at[0 : Z - 1], sems.at[21])
    peaks = jnp.max(mx_z[...], axis=0)
    mx_own[1] = peaks

    def begin_max(i, carry):
        remote(mx_own.at[1], mx_r.at[p], 22, 23, rows=lax.rem(p + i, R)).start()
        return carry

    lax.fori_loop(1, R, begin_max, 0)
    mx_r[p] = peaks
    energy[...] = lax.rsqrt(energy[...])
    drain(mx_r.at[0 : R - 1], sems.at[23])
    drain(mx_r.at[0 : R - 1], sems.at[22])
    drain(mx_z.at[0 : Z - 1], sems.at[20])
    peaks = jnp.sqrt(jnp.max(mx_r[...], axis=0))
    for level in range(3):
        peak = jnp.max(peaks[:, 128 * level : 128 * level + 128], axis=1, keepdims=True)
        energy[level] = jnp.minimum(energy[level] * (fractions[level] * peak), 1.0)

    def shrunk(ch):
        for t in range(4):
            out = energy[0, t] * det[0, ch, t]
            out = out + energy[1, t] * det[1, ch, t]
            ob[ch, :, 128 * t : 128 * t + 128] = out + energy[2, t] * det[2, ch, t]

    block = pl.ds(pl.multiple_of(512 * z, 512), 512)

    def final(i, carry):
        ch = lax.rem(z + 2 - (i // 2) + 2 * (i // 3), Z)
        shrunk(ch)
        remote(ob.at[ch], shrink_ref.at[:, block], 24, 25, chan=ch).start()
        return carry

    lax.fori_loop(1, Z, final, 0)
    shrunk(z)
    own = pltpu.make_async_copy(ob.at[z], shrink_ref.at[:, block], sems.at[28])
    own.start()
    drain(ob.at[0 : Z - 1], sems.at[25])
    drain(ob.at[0 : Z - 1], sems.at[24])
    own.wait()
    blur_out.wait()


def shards(estimate, dirty_image, psf_weights):
    constants = tables()
    arguments = (estimate[0], dirty_image[0], psf_weights[0].T, *constants)
    anywhere = pl.BlockSpec(memory_space=pl.ANY)
    block = jax.ShapeDtypeStruct((64, 2048), F32)
    dma = pltpu.SemaphoreType.DMA
    shapes = [
        (2048, 64),
        (640, 256),
        (R, TILES, 8, 128),
        (R, TILES + 1, 8, 128),
        (3, 256, 256),
        (R, 3, 8, 128),
        (R, 3, 8, 128),
        (R, 3, 8, 128),
        (R, 2, 8, 128),
        (Z, 4, 64, 128),
        (Z, 64, 128),
        (2, Z, 16, 128),
        (2, Z, 16, 128),
        (Z, 5, 112, 128),
        (5, 112, 128),
        (5, 112, 128),
        (5, 112, 128),
        (3, Z, 4, 64, 128),
        (3, 4, 64, 128),
        (Z, 64, 512),
        (2, 1, 384),
        (Z, 1, 384),
        (R, 1, 384),
        (64, 2048),
        (3, 32, 8, 128),
        (2, 32, 8, 128),
        (2, 32, 8, 128),
        (2, 32, 8, 128),
    ]
    shrink, blurred = pl.pallas_call(
        kernel,
        out_shape=(block, block),
        in_specs=[anywhere] * len(arguments),
        out_specs=(anywhere, anywhere),
        scratch_shapes=[pltpu.VMEM(a.shape, a.dtype) for a in arguments]
        + [pltpu.VMEM(shape, F32) for shape in shapes]
        + [dma((len(arguments),)), dma((30,))],
        compiler_params=pltpu.CompilerParams(
            collective_id=0, has_side_effects=True, vmem_limit_bytes=VMEM_LIMIT
        ),
    )(*arguments)
    residual = dirty_image[0] - blurred
    new = estimate[0] + step_size * residual - shrink
    return (new[None], residual[None])


def solution(mesh):
    return jax.shard_map(
        shards,
        mesh=mesh,
        in_specs=(P("chan", "rows", None), P("chan", "rows", None), P("chan", None, "rows")),
        out_specs=(P("chan", "rows", None), P("chan", "rows", None)),
        check_vma=False,
    )
```

```python
import functools
import math

import jax
import jax.numpy as jnp
import numpy as np
from jax import lax
from jax.experimental import pallas as pl
from jax.experimental.pallas import tpu as pltpu
from jax.sharding import PartitionSpec as P

fractions = (0.03, 0.02, 0.015)
step_size = 0.9
MESH = pl.DeviceIdType.MESH
F32 = jnp.float32
BF16 = jnp.bfloat16
R = 32
Z = 4
VMEM_LIMIT = 60 * 1024 * 1024
TILES = 4


def linear(pairs):
    total = None
    for coef, value in pairs:
        if abs(coef) < 1e-12:
            continue
        if abs(coef - 1.0) < 1e-12:
            total = value if total is None else total + value
        elif abs(coef + 1.0) < 1e-12:
            total = -value if total is None else total - value
        else:
            term = coef * value
            total = term if total is None else total + term
    return total


def cosine_16(first, middle, e):
    out = [None] * 9
    for k in range(5):
        even = linear(
            [(1.0, first), (1.0 if k % 2 == 0 else -1.0, middle)]
            + [(math.cos(2 * math.pi * k * a / 16), e[a]) for a in (2, 4, 6)]
        )
        odd = linear([(math.cos(2 * math.pi * k * a / 16), e[a]) for a in (1, 3, 5, 7)])
        if odd is None:
            out[k] = even
            out[8 - k] = even
        else:
            out[k] = even + odd
            out[8 - k] = even - odd
    return out


def sine_16(o):
    out = [None] * 8
    for k in range(1, 5):
        even = linear([(math.sin(2 * math.pi * k * a / 16), o[a]) for a in (2, 4, 6)])
        odd = linear([(math.sin(2 * math.pi * k * a / 16), o[a]) for a in (1, 3, 5, 7)])
        if even is None:
            out[k] = odd
        else:
            out[k] = odd + even
            out[8 - k] = odd - even
    return out


def fft(values, sign):
    count = len(values)
    if count == 1:
        return values
    if count == 2:
        (ar, ai), (br, bi) = values
        return [(ar + br, ai + bi), (ar - br, ai - bi)]
    if count == 4:
        (ar, ai), (br, bi), (cr, ci), (dr, di) = values
        sr, si, tr, ti = ar + cr, ai + ci, ar - cr, ai - ci
        ur, ui, vr, vi = br + dr, bi + di, br - dr, bi - di
        if sign > 0:
            return [(sr + ur, si + ui), (tr - vi, ti + vr), (sr - ur, si - ui), (tr + vi, ti - vr)]
        return [(sr + ur, si + ui), (tr + vi, ti - vr), (sr - ur, si - ui), (tr - vi, ti + vr)]
    quarter = count // 4
    parts = [fft(values[n::4], sign) for n in range(4)]
    out = [None] * count
    for k in range(quarter):
        four = []
        for n in range(4):
            re, im = parts[n][k]
            angle = sign * 2 * math.pi * n * k / count
            c, s = math.cos(angle), math.sin(angle)
            if n * k == 0:
                four.append((re, im))
            elif abs(abs(c) - abs(s)) < 1e-9:
                h = abs(c)
                cs, ss = math.copysign(1, c), math.copysign(1, s)
                r = (re if cs > 0 else -re) - (im if ss > 0 else -im)
                i = (im if cs > 0 else -im) + (re if ss > 0 else -re)
                four.append((h * r, h * i))
            else:
                four.append((re * c - im * s, re * s + im * c))
        for m, value in enumerate(fft(four, sign)):
            out[k + m * quarter] = value
    return out


def split(value):
    high = value.astype(BF16)
    return high, (value - high.astype(F32)).astype(BF16)


def dot3(a, b, dims):
    (ah, al), (bh, bl) = a, b
    dot = functools.partial(
        lax.dot_general, dimension_numbers=(dims, ((), ())), preferred_element_type=F32
    )
    return dot(ah, bh) + (dot(al, bh) + dot(ah, bl))


def tables():
    m = np.arange(128)
    rows = np.zeros((256, 256))
    for d in range(32):
        for jj in range(4):
            angle = 2 * np.pi * ((4 * d + jj) * m % 128) / 128
            rows[8 * d + jj] = np.concatenate([np.cos(angle), np.sin(angle)])
            rows[8 * d + 4 + jj] = np.concatenate([-np.sin(angle), np.cos(angle)])
    n = np.arange(64)
    angle = 2 * np.pi * (n[:, None] * n[None, :] % 64) / 64
    cols = np.zeros((2, 2, 64, 2, 2, 64))
    for kk in range(2):
        cols[0, kk, :, 0, kk] = np.cos(angle)
        cols[1, kk, :, 0, kk] = np.sin(angle)
        cols[0, kk, :, 1, kk] = -np.sin(angle)
        cols[1, kk, :, 1, kk] = np.cos(angle)
    cols = cols.reshape(256, 256)
    early = np.concatenate([np.arange(16), np.arange(48, 64)])
    chunk = np.concatenate([early, np.arange(16, 48)]).reshape(2, 32)
    back = cols.T.reshape(256, 2, 2, 64)[:, :, :, chunk]
    back = back.transpose(0, 1, 3, 2, 4).reshape(256, 256)
    k = np.arange(1, 9)
    angle = -2 * np.pi * k[:, None] * m[None, :] / 2048
    row_twist = np.concatenate([np.cos(angle), np.sin(angle)])
    u1 = np.arange(32)
    angle = -2 * np.pi * u1[:, None] * n[None, :] / 2048
    angle = np.concatenate([angle, angle], axis=1)
    lanes = np.broadcast_to(chunk[:, None, :], (2, 2, 32)).reshape(128)
    turned = -2 * np.pi * u1[:, None] * lanes[None, :] / 2048
    col_twist = np.stack([np.cos(angle), np.sin(angle), np.cos(turned), np.sin(turned)])

    flip = np.zeros((2, 2, 128, 128))
    for kk in range(2):
        for u in range(64):
            flip[0, :, 64 * kk + 63 - u, 64 * kk + u] = 1.0
            flip[1, :, 64 * kk + (64 - u) % 64, 64 * kk + u] = 1.0
    pick = np.zeros((2, 40, 2, 64))
    for kk in range(2):
        for q in range(3):
            for half in range(2):
                s = 4 * q + 2 * half + kk
                k = s + 1 if s < 8 else 0
                for jj in range(4):
                    if s < 9:
                        pick[kk, 8 * q + 4 * half + jj, :, 16 * jj + k] = 2.0**-22
                    if s < 7:
                        pick[kk, 24 + 8 * q + 4 * half + jj, :, 16 * (3 - jj) + 16 - k] = 2.0**-22
    perm = np.concatenate([flip.reshape(512, 128), pick.reshape(80, 128)]).astype(BF16)

    def halves(table):
        high = table.astype(BF16)
        return np.stack([high, (table - high.astype(np.float64)).astype(BF16)])

    real = rows[:, 0:128].reshape(32, 2, 4, 128).transpose(1, 0, 2, 3).reshape(256, 128)
    return (
        halves(real),
        halves(rows),
        halves(cols),
        halves(back),
        np.asarray(row_twist, np.float32),
        np.asarray(col_twist, np.float32),
        perm,
    )


def roll(value, shift, axis):
    return pltpu.roll(value, shift % value.shape[axis], axis)


hops = ((2, 2), (1, 1), (3, 3), (1, 3), (3, 1), (2, 1), (1, 2), (2, 3))
hops = hops + ((3, 2), (2, 0), (0, 2), (1, 0), (0, 1), (3, 0), (0, 3), (0, 0))


def others(p):
    core, x, y = lax.rem(p, 2), lax.rem(p // 2, 4), p // 8
    for far in (0, 1):
        for dy, dx in hops:
            if (dy, dx, far) != (0, 0, 0):
                yield lax.rem(y + dy, 4) * 8 + lax.rem(x + dx, 4) * 2 + lax.rem(core + far, 2)


def drain(ref, sem):
    pltpu.make_async_copy(ref, ref, sem).wait()


def kernel(
    est_in, dirty_in, psf_in, real_table_in, row_table_in, col_table_in, col_back_in, row_twist_in, col_twist_in,
    perm_in,
    shrink_ref, blur_ref,
    est, dirty, psf_wide, real_table, row_table, col_table, col_back, row_twist, col_twist, perm,
    psf, abuf, send, recv, send_8, recv_8, spec, send_a, send_b, recv_a, recv_b, send_9, recv_9,
    hz, hh, hp, hpr, hr, rows_done, smooth_a, smooth_b, det, energy, ob, mx_own, mx_z, mx_r, blur,
    weights, mirror, flipped, mirror_in, in_sems, sems,
):
    z = lax.axis_index("chan")
    p = lax.axis_index("rows")

    barrier = pltpu.get_barrier_semaphore()

    def greet_row(i, carry):
        pl.semaphore_signal(
            barrier, inc=1, device_id={"rows": lax.rem(p + i, R)}, device_id_type=MESH
        )
        return carry

    def greet_chan(i, carry):
        pl.semaphore_signal(
            barrier, inc=1, device_id={"chan": lax.rem(z + i, Z)}, device_id_type=MESH
        )
        return carry

    lax.fori_loop(1, R, greet_row, 0)
    lax.fori_loop(1, Z, greet_chan, 0)

    pairs = (
        (est_in, est), (row_twist_in, row_twist), (row_table_in, row_table), (psf_in, psf_wide),
        (perm_in, perm), (col_twist_in, col_twist), (col_table_in, col_table),
        (col_back_in, col_back), (dirty_in, dirty), (real_table_in, real_table),
    )
    loads = [pltpu.make_async_copy(a, b, in_sems.at[i]) for i, (a, b) in enumerate(pairs)]
    for load in loads:
        load.start()

    def remote(source, target, send_sem, recv_sem, **device):
        return pltpu.make_async_remote_copy(
            src_ref=source,
            dst_ref=target,
            send_sem=sems.at[send_sem],
            recv_sem=sems.at[recv_sem],
            device_id=device,
            device_id_type=MESH,
        )

    abuf[576:640, :] = jnp.zeros((64, 256), F32)
    left = lax.broadcasted_iota(jnp.int32, (8, 128), 1) < 64
    for load in loads[:3]:
        load.wait()

    def rows_forward(g, carry):
        at = pl.ds(pl.multiple_of(8 * g, 8), 8)
        x = [est[at, 128 * a : 128 * a + 128] for a in range(16)]
        e = [None] + [x[a] + x[16 - a] for a in range(1, 8)]
        o = [None] + [x[a] - x[16 - a] for a in range(1, 8)]
        re = cosine_16(x[0], x[8], e)
        im = sine_16(o)
        for k in range(1, 9):
            c = row_twist[k - 1 : k, :]
            s = row_twist[k + 7 : k + 8, :]
            to = pl.ds(pl.multiple_of(64 * (k - 1) + 8 * g, 8), 8)
            if k < 8:
                abuf[to, 0:128] = re[k] * c + im[k] * s
                abuf[to, 128:256] = re[k] * s - im[k] * c
            else:
                abuf[to, 0:128] = re[k] * c
                abuf[to, 128:256] = re[k] * s
        to = pl.ds(pl.multiple_of(512 + 8 * g, 8), 8)
        abuf[to, 0:128] = re[0]
        abuf[to, 128:256] = jnp.zeros((8, 128), F32)
        return carry

    lax.fori_loop(0, 8, rows_forward, 0)
    table = (row_table[0], row_table[1])
    for t in range(TILES):
        out = dot3(table, split(abuf[128 * t : 128 * t + 128, :]), ((1,), (1,)))
        send[:, t] = out.reshape(R, 8, 128)
    out = dot3(table, split(abuf[512:640, :]), ((1,), (1,)))
    for i in range(R):
        value = out[8 * i : 8 * i + 8]
        value = jnp.where(left, value, roll(roll(value, 64, 1), 4, 0))
        send_8[i] = value[0:4]

    left_half = lax.broadcasted_iota(jnp.int32, (40, 128), 1) < 64
    for load in loads[3:5]:
        load.wait()
    for b in range(16):
        psf[128 * b : 128 * b + 128, :] = jnp.transpose(psf_wide[:, 128 * b : 128 * b + 128])
    for i in range(8):
        rows = [psf[pl.ds(4 * i + n, 64, stride=32), :] for n in range(4)]
        high, low = split(jnp.concatenate(rows, axis=0))
        both = jnp.concatenate([high, low], axis=1)
        out = lax.dot_general(
            perm[512:592], both, (((1,), (1,)), ((), ())), preferred_element_type=F32
        )
        for n in range(2):
            a = out[0:40, 128 * n : 128 * n + 128]
            b = out[40:80, 128 * n : 128 * n + 128]
            first = jnp.where(left_half, a, roll(b, 64, 1))
            second = jnp.where(left_half, roll(a, 64, 1), b)
            for u1, value in ((4 * i + 2 * n, first), (4 * i + 2 * n + 1, second)):
                for q in range(3):
                    weights[q, u1] = value[8 * q : 8 * q + 8]
                for q in range(2):
                    mirror[q, u1] = value[24 + 8 * q : 32 + 8 * q]
    for q in range(2):
        high, low = split(mirror[q].reshape(256, 128))
        both = jnp.concatenate([high, low], axis=1)
        out = jnp.dot(both, perm[0:256], preferred_element_type=F32)
        zero = jnp.dot(both[0:16], perm[256:512], preferred_element_type=F32)
        flipped[q, 0] = zero[0:8]
        for u1 in range(1, 32):
            flipped[q, 32 - u1] = out[8 * u1 : 8 * u1 + 8]

    pl.semaphore_wait(barrier, R - 1 + Z - 1)

    for to in others(p):
        remote(send.at[to], recv.at[p], 2, 3, rows=to).start()
    for to in others(p):
        remote(send_8.at[to], recv_8.at[p], 30, 31, rows=to).start()

    def partner(q):
        return remote(flipped.at[q], mirror_in.at[q], 26 + q, q, rows=R - 1 - p)

    partner(0).start()
    partner(1).start()
    recv[p] = send[p]
    recv_8[p] = send_8[p]
    for load in loads[5:]:
        load.wait()
    drain(recv_8.at[0 : R - 1], sems.at[31])
    drain(recv.at[0 : R - 1], sems.at[3])

    upper = lax.broadcasted_iota(jnp.int32, (8, 128), 0) < 4
    even = lax.broadcasted_iota(jnp.int32, (8, 128), 1) // 32 % 2 == 0

    def gathered(q):
        for i in range(R):
            a = recv[i, 2 * q]
            b = recv[i, 2 * q + 1]
            yield (jnp.where(upper, a, roll(b, 4, 0)), jnp.where(upper, roll(a, 4, 0), b))

    def gathered_8():
        none = jnp.zeros((4, 128), F32)
        for i in range(R):
            a = jnp.concatenate([recv_8[i], none], axis=0)
            yield (jnp.where(left, a, 0.0), jnp.where(left, roll(a, 64, 1), 0.0))

    def columns_forward(q, values):
        for u, (re, im) in enumerate(fft(list(values), -1)):
            c = col_twist[0, u : u + 1, :]
            s = col_twist[1, u : u + 1, :]
            spec[q, 8 * u : 8 * u + 8, 0:128] = re * c - im * s
            spec[q, 8 * u : 8 * u + 8, 128:256] = re * s + im * c
        spec[q] = dot3(split(spec[q]), (col_table[0], col_table[1]), ((1,), (0,)))

    def columns_inverse(q, w):
        out = spec[q]
        w = w.reshape(256, 128)
        out = jnp.concatenate([out[:, 0:128] * w, out[:, 128:256] * w], axis=1)
        spec[q] = dot3(split(out), (col_back[0], col_back[1]), ((1,), (0,)))
        values = []
        for u in range(R):
            c = col_twist[2, u : u + 1, :]
            s = col_twist[3, u : u + 1, :]
            re = spec[q, 8 * u : 8 * u + 8, 0:128]
            im = spec[q, 8 * u : 8 * u + 8, 128:256]
            values.append((re * c + im * s, im * c - re * s))
        return fft(values, 1)

    def one_forward(q, carry):
        columns_forward(q, gathered(q))
        return carry

    def one_inverse(q, carry):
        partner(q).wait_recv()
        for i, (re, im) in enumerate(columns_inverse(q, weights[q] + mirror_in[q])):
            a = jnp.where(upper, re, roll(im, 4, 0))
            b = jnp.where(upper, roll(re, 4, 0), im)
            send_a[i, q] = jnp.where(left, a, roll(b, 64, 1))
            send_b[i, q] = jnp.where(left, roll(a, 64, 1), b)
        for to in others(p):
            remote(send_a.at[to, q], recv_a.at[p, q], 4, 5, rows=to).start()
        return carry

    columns_forward(2, gathered_8())
    for i, (re, im) in enumerate(columns_inverse(2, weights[2])):
        send_9[i] = jnp.where(even, re, roll(im, 32, 1))[0:4]
    for to in others(p):
        remote(send_9.at[to], recv_9.at[p], 32, 33, rows=to).start()
    lax.fori_loop(0, 2, one_forward, 0)
    lax.fori_loop(0, 2, one_inverse, 0)
    for to in others(p):
        remote(send_b.at[to], recv_b.at[p], 6, 7, rows=to).start()
    recv_a[p] = send_a[p]
    recv_b[p] = send_b[p]
    recv_9[p] = send_9[p]

    def rows_inverse(base, spread, first, last):
        def group(g, carry):
            re, im = [None] * 9, [None] * 8
            for k in range(1, 9):
                c = row_twist[k - 1 : k, :]
                s = row_twist[k + 7 : k + 8, :]
                to = pl.ds(pl.multiple_of(base + 32 * (k - 1) + 8 * g, 8), 8)
                gr, gi = abuf[to, 0:128], abuf[to, 128:256]
                re[k] = gr * c + gi * s
                if k < 8:
                    im[k] = gi * c - gr * s
            re[0] = abuf[pl.ds(pl.multiple_of(last + 8 * g, 8), 8), 0:128]
            cosine = cosine_16(re[0], re[8], re)
            sine = sine_16(im)
            at = pl.ds(pl.multiple_of(first + 8 * g + spread * (g // 2), 8), 8)
            edges = {}
            for a in range(16):
                if a == 0 or a == 8:
                    blurred = cosine[a]
                elif a < 8:
                    blurred = cosine[a] - sine[a]
                else:
                    blurred = cosine[16 - a] + sine[16 - a]
                lanes = slice(128 * a, 128 * a + 128)
                blur[at, lanes] = blurred
                halfway = est[at, lanes] + step_size * (dirty[at, lanes] - blurred)
                hz[a // 4, a % 4, at, :] = halfway
                if a % 4 in (0, 3):
                    edges[a] = halfway
            none = jnp.zeros((8, 128), F32)
            for c in range(Z):
                after = edges[4 * c + 4] if c < Z - 1 else none
                before = edges[4 * c - 1] if c > 0 else none
                hh[c, at, :] = roll(jnp.where(left, after, before), 16, 1)
            return carry

        lax.fori_loop(0, 4, group, 0)

    lane_16 = lax.broadcasted_iota(jnp.int32, (16, 128), 1)

    def pack(half, groups):
        for c in range(Z):
            a, b = (hh[c, 16 * g : 16 * g + 16, :] for g in groups)
            hp[half, c] = jnp.where(lane_16 < 32, a, roll(b, 32, 1))

    def unpack(half, groups):
        for c in range(Z):
            for e, g in enumerate(groups):
                hr[c, 4, 24 + 16 * g : 40 + 16 * g, :] = roll(hpr[half, c], -32 * e - 16, 1)

    drain(recv_a.at[0 : R - 1], sems.at[5])
    drain(recv_9.at[0 : R - 1], sems.at[33])
    block = split(recv_9[...].reshape(128, 128))
    real, imag = (
        dot3(block, (real_table[0, at : at + 128], real_table[1, at : at + 128]), ((0,), (0,)))
        for at in (0, 128)
    )
    abuf[256:288, 0:128] = real[0:32] + imag[32:64]
    abuf[320:352, 0:128] = real[64:96] + imag[96:128]
    for t in range(2):
        block = recv_a[:, t].reshape(256, 128)
        abuf[128 * t : 128 * t + 128, :] = dot3(split(block), table, ((0,), (0,)))
    rows_inverse(0, 32, 0, 256)
    pack(0, (0, 3))
    for i in (2, 1, 3):
        to = lax.rem(z + i, Z)
        for r in (0, 48):
            remote(
                hz.at[to, :, r : r + 16], hr.at[z, 0:4, r + 24 : r + 40], 8, 9, chan=to
            ).start()
        remote(hp.at[0, to], hpr.at[0, z], 10, 11, chan=to).start()

    drain(recv_b.at[0 : R - 1], sems.at[7])
    for t in range(2):
        block = recv_b[:, t].reshape(256, 128)
        abuf[384 + 128 * t : 512 + 128 * t, :] = dot3(split(block), table, ((0,), (0,)))
    rows_inverse(384, 0, 16, 320)
    pack(1, (1, 2))
    blur_out = pltpu.make_async_copy(blur, blur_ref, sems.at[29])
    blur_out.start()
    for i in (2, 1, 3):
        to = lax.rem(z + i, Z)
        remote(hz.at[to, :, 16:48], hr.at[z, 0:4, 40:72], 12, 13, chan=to).start()
        remote(hp.at[1, to], hpr.at[1, z], 14, 15, chan=to).start()
    hr[z, 0:4, 24:88] = hz[z]
    hpr[:, z] = hp[:, z]

    hr[:, :, 0:8, :] = jnp.zeros((Z, 5, 8, 128), F32)
    hr[:, :, 104:112, :] = jnp.zeros((Z, 5, 8, 128), F32)

    @pl.when(p == 0)
    def _():
        hr[:, :, 8:24, :] = jnp.zeros((Z, 5, 16, 128), F32)

    @pl.when(p == R - 1)
    def _():
        hr[:, :, 88:104, :] = jnp.zeros((Z, 5, 16, 128), F32)

    drain(hz.at[0 : Z - 1, :, 0:32], sems.at[9])
    drain(hp.at[0, 0 : Z - 1], sems.at[11])
    unpack(0, (0, 3))
    above = remote(hr.at[:, :, 24:40], hr.at[:, :, 88:104], 16, 17, rows=lax.rem(p + R - 1, R))
    below = remote(hr.at[:, :, 72:88], hr.at[:, :, 8:24], 18, 19, rows=lax.rem(p + 1, R))

    @pl.when(p > 0)
    def _():
        above.start()

    @pl.when(p < R - 1)
    def _():
        below.start()

    drain(hz.at[0 : Z - 1, :, 0:32], sems.at[13])
    drain(hp.at[0, 0 : Z - 1], sems.at[15])
    unpack(1, (1, 2))

    @pl.when(p < R - 1)
    def _():
        above.wait_recv()

    @pl.when(p > 0)
    def _():
        below.wait_recv()


    lane_8 = lax.broadcasted_iota(jnp.int32, (8, 128), 1)
    top = jnp.where(p > 0, 1.0, 0.0)
    bottom = jnp.where(p < R - 1, 1.0, 0.0)
    side = jnp.where(
        lane_8 < 64, jnp.where(z < Z - 1, 1.0, 0.0), jnp.where(z > 0, 1.0, 0.0)
    )

    row_8 = lax.broadcasted_iota(jnp.int32, (8, 128), 0)

    def down(x, spacing):
        count = len(x)
        half = [roll(v, 4, 0) for v in x] if spacing > 1 else None
        if spacing > 1:
            half = (
                [half[0]]
                + [jnp.where(row_8 < 4, half[i - 1], half[i]) for i in range(1, count)]
                + [half[-1]]
            )
        if spacing == 4:
            return [None] + [
                (x[i - 1] + x[i + 1]) * (1 / 256)
                + (x[i] * (6 / 256) + (half[i] + half[i + 1]) * (4 / 256))
                for i in range(1, count - 1)
            ]
        if spacing == 2:
            plus = [roll(v, 2, 0) for v in x]
            minus = [roll(v, -2, 0) for v in x]
            out = []
            for i in range(count):
                above = jnp.where(row_8 < 2, plus[max(i - 1, 0)], plus[i])
                below = jnp.where(row_8 >= 6, minus[min(i + 1, count - 1)], minus[i])
                out.append(
                    (half[i] + half[i + 1]) * (1 / 256)
                    + (x[i] * (6 / 256) + (above + below) * (4 / 256))
                )
            return out
        shifted = {}
        for k in (1, -1, 2, -2):
            turned = [roll(v, k, 0) for v in x]
            if k > 0:
                shifted[k] = [
                    jnp.where(row_8 < k, turned[max(i - 1, 0)], turned[i]) for i in range(count)
                ]
            else:
                shifted[k] = [
                    jnp.where(row_8 >= 8 + k, turned[min(i + 1, count - 1)], turned[i])
                    for i in range(count)
                ]
        return [
            (shifted[2][i] + shifted[-2][i]) * (1 / 256)
            + (x[i] * (6 / 256) + (shifted[1][i] + shifted[-1][i]) * (4 / 256))
            for i in range(count)
        ]

    def along(x, spacing):
        total = []
        rolled = {k: [roll(v, k * spacing, 1) for v in x] for k in (1, -1, 2, -2)}
        for t in range(5):
            near = jnp.where(lane_8 < spacing, rolled[1][t - 1], rolled[1][t]) + jnp.where(
                lane_8 >= 128 - spacing, rolled[-1][(t + 1) % 5], rolled[-1][t]
            )
            far = jnp.where(lane_8 < 2 * spacing, rolled[2][t - 1], rolled[2][t]) + jnp.where(
                lane_8 >= 128 - 2 * spacing, rolled[-2][(t + 1) % 5], rolled[-2][t]
            )
            total.append(6.0 * x[t] + (4.0 * near + far))
        return total

    def starlet(ch, carry):
        for level, (start, stop) in enumerate(((0, 12), (1, 11), (2, 10))):
            source = (hr.at[ch], smooth_a, smooth_b)[level]
            target = (smooth_a, smooth_b, None)[level]
            first, last = ((0, 12), (0, 12), (1, 11))[level]
            for t in range(5):
                x = [source[t, 8 * i + 8 : 8 * i + 16, :] for i in range(first, last)]
                x = down(x, 1 << level)
                for i in range(start, stop):
                    rows_done[t, 8 * i + 8 : 8 * i + 16, :] = x[i - first]
            for i in range(start, stop):
                rows = slice(8 * i + 8, 8 * i + 16)
                x = along([rows_done[t, rows, :] for t in range(5)], 1 << level)
                if target is not None:
                    if i < 2:
                        x = [v * top for v in x]
                    if i >= 10:
                        x = [v * bottom for v in x]
                    x[4] = x[4] * side
                    for t in range(5):
                        target[t, rows, :] = x[t]
                if 2 <= i < 10:
                    at = slice(8 * i - 16, 8 * i - 8)
                    for t in range(4):
                        detail = source[t, rows, :] - x[t]
                        det[level, ch, t, at, :] = detail
                        energy[level, t, at, :] = energy[level, t, at, :] + detail * detail
        return carry

    energy[...] = jnp.zeros((3, 4, 64, 128), F32)
    lax.fori_loop(0, Z, starlet, 0)

    peaks = jnp.concatenate(
        [
            jnp.max(jnp.max(energy[level], axis=0), axis=0, keepdims=True)
            for level in range(3)
        ],
        axis=1,
    )
    mx_own[0] = peaks
    for i in range(1, Z):
        remote(mx_own.at[0], mx_z.at[z], 20, 21, chan=lax.rem(z + i, Z)).start()
    mx_z[z] = peaks
    drain(mx_z.at[0 : Z - 1], sems.at[21])
    peaks = jnp.max(mx_z[...], axis=0)
    mx_own[1] = peaks

    def begin_max(i, carry):
        remote(mx_own.at[1], mx_r.at[p], 22, 23, rows=lax.rem(p + i, R)).start()
        return carry

    lax.fori_loop(1, R, begin_max, 0)
    mx_r[p] = peaks
    energy[...] = lax.rsqrt(energy[...])
    drain(mx_r.at[0 : R - 1], sems.at[23])
    peaks = jnp.sqrt(jnp.max(mx_r[...], axis=0))
    for level in range(3):
        peak = jnp.max(peaks[:, 128 * level : 128 * level + 128], axis=1, keepdims=True)
        energy[level] = jnp.minimum(energy[level] * (fractions[level] * peak), 1.0)

    def shrunk(ch):
        for t in range(4):
            out = energy[0, t] * det[0, ch, t]
            out = out + energy[1, t] * det[1, ch, t]
            ob[ch, :, 128 * t : 128 * t + 128] = out + energy[2, t] * det[2, ch, t]

    block = pl.ds(pl.multiple_of(512 * z, 512), 512)

    def final(i, carry):
        ch = lax.rem(z + 2 - (i // 2) + 2 * (i // 3), Z)
        shrunk(ch)
        remote(ob.at[ch], shrink_ref.at[:, block], 24, 25, chan=ch).start()
        return carry

    lax.fori_loop(1, Z, final, 0)
    shrunk(z)
    own = pltpu.make_async_copy(ob.at[z], shrink_ref.at[:, block], sems.at[28])
    own.start()
    drain(send_8.at[0 : R - 1], sems.at[30])
    drain(send.at[0 : R - 1], sems.at[2])
    partner(0).wait_send()
    partner(1).wait_send()
    drain(send_a.at[0 : R - 1], sems.at[4])
    drain(send_b.at[0 : R - 1], sems.at[6])
    drain(send_9.at[0 : R - 1], sems.at[32])
    drain(hz.at[0 : Z - 1, :, 0:32], sems.at[8])
    drain(hp.at[0, 0 : Z - 1], sems.at[10])
    drain(hz.at[0 : Z - 1, :, 0:32], sems.at[12])
    drain(hp.at[0, 0 : Z - 1], sems.at[14])

    @pl.when(p > 0)
    def _():
        above.wait_send()

    @pl.when(p < R - 1)
    def _():
        below.wait_send()

    drain(mx_r.at[0 : R - 1], sems.at[22])
    drain(mx_z.at[0 : Z - 1], sems.at[20])
    drain(ob.at[0 : Z - 1], sems.at[25])
    drain(ob.at[0 : Z - 1], sems.at[24])
    own.wait()
    blur_out.wait()


def shards(estimate, dirty_image, psf_weights):
    constants = tables()
    arguments = (estimate[0], dirty_image[0], psf_weights[0].T, *constants)
    anywhere = pl.BlockSpec(memory_space=pl.ANY)
    block = jax.ShapeDtypeStruct((64, 2048), F32)
    dma = pltpu.SemaphoreType.DMA
    shapes = [
        (2048, 64),
        (640, 256),
        (R, TILES, 8, 128),
        (R, TILES, 8, 128),
        (R, 4, 128),
        (R, 4, 128),
        (3, 256, 256),
        (R, 2, 8, 128),
        (R, 2, 8, 128),
        (R, 2, 8, 128),
        (R, 2, 8, 128),
        (R, 4, 128),
        (R, 4, 128),
        (Z, 4, 64, 128),
        (Z, 64, 128),
        (2, Z, 16, 128),
        (2, Z, 16, 128),
        (Z, 5, 112, 128),
        (5, 112, 128),
        (5, 112, 128),
        (5, 112, 128),
        (3, Z, 4, 64, 128),
        (3, 4, 64, 128),
        (Z, 64, 512),
        (2, 1, 384),
        (Z, 1, 384),
        (R, 1, 384),
        (64, 2048),
        (3, 32, 8, 128),
        (2, 32, 8, 128),
        (2, 32, 8, 128),
        (2, 32, 8, 128),
    ]
    shrink, blurred = pl.pallas_call(
        kernel,
        out_shape=(block, block),
        in_specs=[anywhere] * len(arguments),
        out_specs=(anywhere, anywhere),
        scratch_shapes=[pltpu.VMEM(a.shape, a.dtype) for a in arguments]
        + [pltpu.VMEM(shape, F32) for shape in shapes]
        + [dma((len(arguments),)), dma((34,))],
        compiler_params=pltpu.CompilerParams(
            collective_id=0, has_side_effects=True, vmem_limit_bytes=VMEM_LIMIT
        ),
    )(*arguments)
    residual = dirty_image[0] - blurred
    new = estimate[0] + step_size * residual - shrink
    return (new[None], residual[None])


def solution(mesh):
    return jax.shard_map(
        shards,
        mesh=mesh,
        in_specs=(P("chan", "rows", None), P("chan", "rows", None), P("chan", None, "rows")),
        out_specs=(P("chan", "rows", None), P("chan", "rows", None)),
        check_vma=False,
    )
```
